32 devices in a mesh: fsdp: 2 (over x), ctx: 4 (over z), tp: 4 (over y, core).
Axes of the slice: x: 2, y: 2, z: 4, core: 2. Of those that a mesh axis runs over, the one named last changes fastest.
Arguments:
- tokens: bfloat16 [8192, 1024], P(('fsdp', 'ctx')), may hold values from -6 to 6
- w_qkv: bfloat16 [3, 1024, 1024], P(None, 'fsdp', 'tp'), may hold values from -0.25 to 0.25
- w_out: bfloat16 [1024, 1024], P('tp', 'fsdp'), may hold values from -0.75 to 0.75
- w_up: bfloat16 [1024, 4096], P('fsdp', 'tp'), may hold values from -0.1875 to 0.1875
- w_down: bfloat16 [4096, 1024], P('tp', 'fsdp'), may hold values from -0.09375 to 0.09375
- gains: bfloat16 [2, 1024], P(None, 'fsdp'), may hold values from 0.5 to 1.5
- shifts: bfloat16 [2, 1024], P(None, 'fsdp'), may hold values from -3 to 3
- lengths: int32 [2, 3], P('fsdp'), may hold values from 256 to 2048, as said below
- out_grad: bfloat16 [8192, 1024], P(('fsdp', 'ctx')), may hold values from -6 to 6
Outputs:
- out: bfloat16 [8192, 1024], P(('fsdp', 'ctx'))
- input_grad: bfloat16 [8192, 1024], P(('fsdp', 'ctx'))
- grad_qkv: float32 [3, 1024, 1024], P(None, 'fsdp', 'tp')
- grad_out: float32 [1024, 1024], P('tp', 'fsdp')
- grad_up: float32 [1024, 4096], P('fsdp', 'tp')
- grad_down: float32 [4096, 1024], P('tp', 'fsdp')
- grad_gains: float32 [2, 1024], P(None, 'fsdp')
- grad_shifts: float32 [2, 1024], P(None, 'fsdp')
The draws below stay inside these ranges and needn't reach their ends.
Inputs may be any that keep to these rules, and one draw needn't show every extreme that they name: `lengths`: in each row one sequence has exactly 2048 tokens and the others 2048 // 8 to 1024; sequences lie end to end from the pack's first slot, and the slots after them up to 4096 are padding.
All inputs are finite; a program needn't handle non-finite values.
Results may differ from the reference program's by a relative error of at most 0.014.
The reference program's roundings to bfloat16 on the way count: a program that leaves them out, or rounds other values in their place, can miss the bound.
Values may be sent and summed in bfloat16 or wider, within the bound.
No kernel may reach another device: no remote copies, remote signals or barrier semaphores. Data moves between devices by JAX's collectives and lax.ppermute only.
A program may use at most 192 MiB of HBM per device.

```python
import math
import jax
import jax.numpy as jnp
from jax import lax

D = 1024
HEADS = 16
HEAD_DIM = 64
FF = 4096
SEQS = 3
PACK = 4096
SEQ_MAX = 2048
PACKS = 2
TOKENS = 8192


def draw_lengths(key, part):
    longest = jax.random.randint(jax.random.fold_in(key, 11), (PACKS, 1), 0, SEQS)
    shorter = jax.random.randint(jax.random.fold_in(key, 12), (PACKS, SEQS), SEQ_MAX // 8, SEQ_MAX // 2 + 1)
    places = jnp.arange(SEQS, dtype=jnp.int32)[None, :]
    return jnp.where(places == longest, SEQ_MAX, shorter).astype(jnp.int32)


def shard_levels(stream_key, shape, pieces, smallest, largest):
    def one(axis_at, parts):
        steps = jax.random.uniform(jax.random.fold_in(jax.random.fold_in(stream_key, 6), axis_at), (parts,), jnp.float32, smallest / len(pieces), largest / len(pieces))
        return jnp.repeat(jnp.exp(steps), shape[axis_at] // parts).reshape((-1,) + (1,) * (len(shape) - axis_at - 1))

    level = one(*pieces[0])
    for cut in pieces[1:]:
        level = level * one(*cut)
    return level


def bell_draw(key, extent, deviation, limit, shards=(), kind=jnp.bfloat16):
    drawn = jax.random.normal(key, extent, jnp.float32) * deviation
    if len(shards) > 0:
        drawn = shard_levels(key, extent, shards, -0.22, 0.18) * drawn
    return jnp.clip(drawn, min=-limit, max=limit).astype(kind)


def setup_inputs(seed: int = 0) -> dict:
    streams_of = jax.random.split(jax.random.key(seed), 10)
    return {
        "tokens": bell_draw(streams_of[0], (TOKENS, D), 1.0, 6.0, ((0, 8),)),
        "w_qkv": bell_draw(streams_of[1], (3, D, D), (D // 2) ** -0.5, 0.25, ((1, 2), (2, 4))),
        "w_out": bell_draw(streams_of[2], (D, D), (D // 16) ** -0.5, 0.75, ((0, 4), (1, 2))),
        "w_up": bell_draw(streams_of[3], (D, FF), D ** -0.5, 0.1875, ((0, 2), (1, 4))),
        "w_down": bell_draw(streams_of[4], (FF, D), FF ** -0.5, 0.09375, ((0, 4), (1, 2))),
        "gains": jnp.clip(1.0 + 0.1 * jax.random.normal(streams_of[5], (2, D), jnp.float32), 0.5, 1.5).astype(jnp.bfloat16),
        "shifts": bell_draw(streams_of[6], (2, D), 0.5, 3.0, ((1, 2),)),
        "lengths": draw_lengths(jax.random.fold_in(streams_of[9], 71), 0),
        "out_grad": bell_draw(streams_of[8], (TOKENS, D), 1.0, 6.0, ((0, 8),)),
    }


@jax.custom_vjp
def low(v):
    return lax.optimization_barrier(v.astype(jnp.bfloat16)).astype(jnp.float32)

@jax.custom_vjp
def low_back(v):
    return v

def low_keep(v):
    return (low(v), None)

def low_pass(kept, grad):
    return (grad,)

def back_keep(v):
    return (v, None)

def back_low(kept, grad):
    return (low(grad),)
low.defvjp(low_keep, low_pass)
low_back.defvjp(back_keep, back_low)
precise = lax.Precision.HIGHEST
norm_eps = 1e-12
masked_low = -1e+30

def both_round(value):
    return low_back(low(value))

def product(left, right):
    return jnp.dot(left, right, precision=precise, preferred_element_type=jnp.float32)

def layer_norm(rows, gain, shift):
    centre = rows - lax.optimization_barrier(jnp.mean(rows, axis=-1, keepdims=True))
    spread = lax.optimization_barrier(jnp.mean(centre * centre, axis=-1, keepdims=True))
    return centre * lax.rsqrt(spread + norm_eps) * gain + shift

def segment_of(lengths_row, total):
    seq_ends = jnp.cumsum(lengths_row)
    positions = jnp.arange(total, dtype=jnp.int32)
    return lax.optimization_barrier(jnp.sum((positions[:, None] >= seq_ends[None, :]).astype(jnp.int32), axis=1)).astype(jnp.int32)

def attention(queries, key_rows, value_rows, segment):
    block_rows = min(512, PACK)
    block_count = PACK // block_rows
    score_scale = 1.0 / math.sqrt(HEAD_DIM)
    query_heads = queries.reshape(block_count, block_rows, HEADS, HEAD_DIM)
    seg_blocks = segment.reshape(block_count, block_rows)
    key_heads = key_rows.reshape(PACK, HEADS, HEAD_DIM)
    value_heads = value_rows.reshape(PACK, HEADS, HEAD_DIM)

    def one_block(inputs):
        query_block, seg_block = inputs
        raw_scores = low_back(jnp.einsum('qhd,khd->hqk', query_block, key_heads, precision=precise))
        scores = raw_scores * score_scale
        allowed = (seg_block[:, None] == segment[None, :]) & (segment[None, :] < SEQS)
        has_key = jnp.any(allowed, axis=1)
        masked = jnp.where(allowed[None], scores, masked_low)
        row_max = jnp.where(has_key[None, :, None], lax.optimization_barrier(jnp.max(masked, axis=2, keepdims=True)), 0.0)
        exp_terms = jnp.where(allowed[None], jnp.exp(masked - row_max), 0.0)
        denominator = lax.optimization_barrier(jnp.sum(exp_terms, axis=2, keepdims=True)) + (1.0 - has_key.astype(jnp.float32))[None, :, None]
        attn_probs = low(exp_terms / denominator)
        return jnp.einsum('hqk,khd->qhd', attn_probs, value_heads, precision=precise)
    context = lax.map(jax.checkpoint(one_block), (query_heads, seg_blocks))
    return context.reshape(PACK, HEADS * HEAD_DIM)

def forward(inputs_f, w_qkv, w_out, w_up, w_down, gains, shifts, segment):
    queries = both_round(product(inputs_f, w_qkv[0]))
    key_rows = both_round(product(inputs_f, w_qkv[1]))
    value_rows = both_round(product(inputs_f, w_qkv[2]))
    context = both_round(attention(queries, key_rows, value_rows, segment))
    attn_out = low_back(product(context, w_out))
    hidden = layer_norm(inputs_f + attn_out, gains[0], shifts[0])
    pre_act = low_back(product(low(hidden), w_up))
    act_low = low(jax.nn.gelu(pre_act, approximate=False))
    ffn_out = low_back(product(act_low, w_down))
    return layer_norm(hidden + ffn_out, gains[1], shifts[1])

def reference(tokens, w_qkv, w_out, w_up, w_down, gains, shifts, lengths, out_grad):
    params = tuple((weight.astype(jnp.float32) for weight in (w_qkv, w_out, w_up, w_down, gains, shifts)))
    pack_rows = tokens.astype(jnp.float32).reshape(PACKS, PACK, D)
    pack_grads = out_grad.astype(jnp.float32).reshape(PACKS, PACK, D)
    totals = tuple((jnp.zeros(weight.shape, jnp.float32) for weight in params))

    def one_pack(sums, inputs):
        inputs_f, cotangent, lengths_row = inputs
        segment = segment_of(lengths_row, PACK)

        def run(rows, *weights):
            return forward(rows, *weights, segment)
        result, pull_back = jax.vjp(run, inputs_f, *params)
        gradients = pull_back(cotangent)
        sums = tuple((before + after for before, after in zip(sums, gradients[1:])))
        return (sums, (result.astype(jnp.bfloat16), gradients[0].astype(jnp.bfloat16)))
    totals, (results, input_grads) = lax.scan(one_pack, totals, (pack_rows, pack_grads, lengths))
    return (results.reshape(TOKENS, D), input_grads.reshape(TOKENS, D), totals[0], totals[1], totals[2], totals[3], totals[4], totals[5])
```

```python
import functools
import math

import jax
import jax.numpy as jnp
from jax import lax
from jax.experimental import pallas as pl
from jax.experimental.pallas import tpu as pltpu
from jax.sharding import PartitionSpec as P

HEAD_DIM = 64
BLK = 256
LOW = -1e30
norm_eps = 1e-12
f32 = jnp.float32
bf16 = jnp.bfloat16


def contract(left, right, left_dim, right_dim):
    return lax.dot_general(
        left, right, (((left_dim,), (right_dim,)), ((), ())), preferred_element_type=f32
    )


def nn(left, right):
    return contract(left, right, 1, 0)


def nt(left, right):
    return contract(left, right, 1, 1)


def tn(left, right):
    return contract(left, right, 0, 0)


def row_limits(info, qbase, rows):
    end0, end1, end2 = info[0], info[1], info[2]
    pos = qbase + lax.broadcasted_iota(jnp.int32, (1, rows), 1)
    first = jnp.where(pos < end0, 0, jnp.where(pos < end1, end0, end1))
    last = jnp.where(pos < end0, end0, jnp.where(pos < end1, end1, end2))
    real = pos < end2
    return jnp.where(real, first, 0), jnp.where(real, last, 0), real


def key_range(info, qbase, rows):
    end0, end1, end2 = info[0], info[1], info[2]
    low = jnp.where(
        qbase < end0,
        0,
        jnp.where(qbase < end1, end0, jnp.where(qbase < end2, end1, 1 << 30)),
    )
    final = qbase + rows - 1
    high = jnp.where(final < end0, end0, jnp.where(final < end1, end1, end2))
    return low, high


def attend_kernel(
    heads, qcount, kcount, info, q_ref, k_ref, vt_ref, ctx_ref, lse_ref, m_sc, l_sc, acc_sc, qm_sc
):
    i = pl.program_id(0)
    rows = q_ref.shape[0]
    qbase = info[3 + i]
    first, last, real = row_limits(info, qbase, rows)
    low, high = key_range(info, qbase, rows)
    factor = math.log2(math.e) / math.sqrt(HEAD_DIM)
    m_sc[...] = jnp.full_like(m_sc, LOW)
    l_sc[...] = jnp.zeros_like(l_sc)
    acc_sc[...] = jnp.zeros_like(acc_sc)
    q = q_ref[...]
    head_of = lax.broadcasted_iota(jnp.int32, q.shape, 1) // HEAD_DIM
    for h in range(heads):
        qm_sc[h * rows : (h + 1) * rows, :] = jnp.where(head_of == h, q, jnp.zeros_like(q))

    def step(j, carry):
        base = info[3 + qcount + j]

        @pl.when((base + BLK > low) & (base < high))
        def _():
            span = pl.ds(pl.multiple_of(j * BLK, BLK), BLK)
            kb = k_ref[span, :]
            vt = vt_ref[:, span]
            posk = base + lax.broadcasted_iota(jnp.int32, (BLK, rows), 0)
            allowed = (posk >= first) & (posk < last)
            for h in range(heads):
                feats = slice(h * HEAD_DIM, (h + 1) * HEAD_DIM)
                s = nt(kb, qm_sc[h * rows : (h + 1) * rows, :])
                s = jnp.where(allowed, s * factor, LOW)
                m_old = m_sc[h : h + 1, :]
                m_new = jnp.maximum(m_old, jnp.max(s, axis=0, keepdims=True))
                p = jnp.exp2(s - m_new)
                alpha = jnp.exp2(m_old - m_new)
                l_sc[h : h + 1, :] = l_sc[h : h + 1, :] * alpha + jnp.sum(p, axis=0, keepdims=True)
                m_sc[h : h + 1, :] = m_new
                acc_sc[feats, :] = acc_sc[feats, :] * alpha + nn(vt[feats, :], p.astype(bf16))

        return carry

    lax.fori_loop(0, kcount, step, 0)
    for h in range(heads):
        feats = slice(h * HEAD_DIM, (h + 1) * HEAD_DIM)
        total = l_sc[h : h + 1, :]
        acc_sc[feats, :] = jnp.where(real, acc_sc[feats, :] / total, 0.0)
        lse_ref[h : h + 1, :] = jnp.where(real, m_sc[h : h + 1, :] + jnp.log2(total), -LOW)
    ctx_ref[...] = acc_sc[...].T.astype(bf16)


def whole(shape):
    return pl.BlockSpec(shape, lambda i, *_: (0,) * len(shape))


def attend(info, q, k, vt):
    rows, width = q.shape
    heads = width // HEAD_DIM
    keys = k.shape[0]
    qcount, kcount = rows // BLK, keys // BLK
    block = pl.BlockSpec((BLK, width), lambda i, *_: (i, 0))
    return pl.pallas_call(
        functools.partial(attend_kernel, heads, qcount, kcount),
        grid_spec=pltpu.PrefetchScalarGridSpec(
            num_scalar_prefetch=1,
            grid=(qcount,),
            in_specs=[block, whole((keys, width)), whole((width, keys))],
            out_specs=[block, pl.BlockSpec((heads, BLK), lambda i, *_: (0, i))],
            scratch_shapes=[
                pltpu.VMEM((heads, BLK), f32),
                pltpu.VMEM((heads, BLK), f32),
                pltpu.VMEM((width, BLK), f32),
                pltpu.VMEM((heads * BLK, width), bf16),
            ],
        ),
        out_shape=[
            jax.ShapeDtypeStruct((rows, width), bf16),
            jax.ShapeDtypeStruct((heads, rows), f32),
        ],
        cost_estimate=pl.CostEstimate(
            flops=8 * rows * keys * width,
            bytes_accessed=4 * keys * width,
            transcendentals=rows * keys * heads // 2,
        ),
        name="attend",
    )(info, q, k, vt)


def attend_back_kernel(
    heads, qcount, kcount, info, q_ref, do_ref, o_ref, lse_ref, k_ref, v_ref, kt_ref,
    dq_ref, own_ref, left_ref, right_ref, far_ref,
    dk_sc, dv_sc, dqt_sc, qm_sc, dom_sc, p_sc, ds_sc, delta_sc,
):
    i = pl.program_id(0)
    rows = q_ref.shape[0]
    qbase = info[3 + i]
    first, last, real = row_limits(info, qbase, rows)
    low, high = key_range(info, qbase, rows)
    scale = 1.0 / math.sqrt(HEAD_DIM)
    factor = math.log2(math.e) * scale

    @pl.when(i == 0)
    def _():
        dk_sc[...] = jnp.zeros_like(dk_sc)
        dv_sc[...] = jnp.zeros_like(dv_sc)

    dqt_sc[...] = jnp.zeros_like(dqt_sc)
    q = q_ref[...]
    do = do_ref[...]
    head_of = lax.broadcasted_iota(jnp.int32, q.shape, 1) // HEAD_DIM
    for h in range(heads):
        qm_sc[h * rows : (h + 1) * rows, :] = jnp.where(head_of == h, q, jnp.zeros_like(q))
        dom_sc[h * rows : (h + 1) * rows, :] = jnp.where(head_of == h, do, jnp.zeros_like(do))
    prod = (do.astype(f32) * o_ref[...].astype(f32)).T
    for h in range(heads):
        delta_sc[h : h + 1, :] = jnp.sum(
            prod[h * HEAD_DIM : (h + 1) * HEAD_DIM, :], axis=0, keepdims=True
        )

    def step(j, carry):
        base = info[3 + qcount + j]

        @pl.when((base + BLK > low) & (base < high))
        def _():
            span = pl.ds(pl.multiple_of(j * BLK, BLK), BLK)
            kb = k_ref[span, :]
            vb = v_ref[span, :]
            kt = kt_ref[:, span]
            posk = base + lax.broadcasted_iota(jnp.int32, (BLK, rows), 0)
            allowed = (posk >= first) & (posk < last)
            for h in range(heads):
                feats = slice(h * HEAD_DIM, (h + 1) * HEAD_DIM)
                cols = slice(h * rows, (h + 1) * rows)
                s = nt(kb[:, feats], q_ref[:, feats])
                dp = nt(vb[:, feats], do_ref[:, feats])
                p = jnp.where(allowed, jnp.exp2(s * factor - lse_ref[h : h + 1, :]), 0.0)
                ds = (p * (dp - delta_sc[h : h + 1, :])).astype(bf16)
                p_sc[:, cols] = p.astype(bf16)
                ds_sc[:, cols] = ds
                dqt_sc[feats, :] += nn(kt[feats, :], ds)
            dv_sc[span, :] += nn(p_sc[...], dom_sc[...])
            dk_sc[span, :] += nn(ds_sc[...], qm_sc[...])

        return carry

    lax.fori_loop(0, kcount, step, 0)
    dq_ref[...] = (dqt_sc[...] * scale).T.astype(bf16)

    @pl.when(i == pl.num_programs(0) - 1)
    def _():
        part = own_ref.shape[1]
        for n, out_ref in enumerate((own_ref, left_ref, right_ref, far_ref)):
            out_ref[0] = (dk_sc[n * part : (n + 1) * part, :] * scale).astype(bf16)
            out_ref[1] = dv_sc[n * part : (n + 1) * part, :].astype(bf16)


def attend_back(info, q, do, o, lse, k, v, kt):
    rows, width = q.shape
    heads = width // HEAD_DIM
    keys = k.shape[0]
    qcount, kcount = rows // BLK, keys // BLK
    block = pl.BlockSpec((BLK, width), lambda i, *_: (i, 0))
    pair = (2, keys // 4, width)
    return pl.pallas_call(
        functools.partial(attend_back_kernel, heads, qcount, kcount),
        grid_spec=pltpu.PrefetchScalarGridSpec(
            num_scalar_prefetch=1,
            grid=(qcount,),
            in_specs=[
                block,
                block,
                block,
                pl.BlockSpec((heads, BLK), lambda i, *_: (0, i)),
                whole((keys, width)),
                whole((keys, width)),
                whole((width, keys)),
            ],
            out_specs=[block] + [whole(pair)] * 4,
            scratch_shapes=[
                pltpu.VMEM((keys, width), f32),
                pltpu.VMEM((keys, width), f32),
                pltpu.VMEM((width, BLK), f32),
                pltpu.VMEM((heads * BLK, width), bf16),
                pltpu.VMEM((heads * BLK, width), bf16),
                pltpu.VMEM((BLK, heads * BLK), bf16),
                pltpu.VMEM((BLK, heads * BLK), bf16),
                pltpu.VMEM((heads, BLK), f32),
            ],
        ),
        out_shape=[jax.ShapeDtypeStruct((rows, width), bf16)]
        + [jax.ShapeDtypeStruct(pair, bf16)] * 4,
        cost_estimate=pl.CostEstimate(
            flops=20 * rows * keys * width,
            bytes_accessed=8 * keys * width,
            transcendentals=rows * keys * heads // 2,
        ),
        name="attend_back",
    )(info, q, do, o, lse, k, v, kt)


def tp_swap(x, bit):
    return lax.ppermute(x, "tp", [(i, i ^ bit) for i in range(4)])


def after(x, *others):
    return lax.optimization_barrier((x,) + others)[0]


def fsdp_whole(shard, dim):
    if lax.axis_size("fsdp") != 2:
        return lax.all_gather(shard, "fsdp", axis=dim, tiled=True)
    other = lax.ppermute(shard, "fsdp", [(0, 1), (1, 0)])
    low_half = lax.axis_index("fsdp") == 0
    return jnp.concatenate(
        [jnp.where(low_half, shard, other), jnp.where(low_half, other, shard)], axis=dim
    )


def fsdp_total(block_of, size, dim):
    count = lax.axis_size("fsdp")
    if count != 2:
        return lax.psum_scatter(block_of(0, size), "fsdp", scatter_dimension=dim, tiled=True)
    half = size // 2
    mine = lax.axis_index("fsdp")
    sent = block_of((1 - mine) * half, half).astype(bf16)
    got = lax.ppermute(sent, "fsdp", [(0, 1), (1, 0)])
    return block_of(mine * half, half) + got.astype(f32)


def ctx_total(terms):
    place = lax.axis_index("ctx")
    sent = terms.astype(bf16)
    got = lax.ppermute(sent, "ctx", [(0, 1), (3, 2)])
    side = lax.optimization_barrier((terms + got.astype(f32)).astype(bf16))
    across = lax.ppermute(side, "ctx", [(1, 2), (2, 1)])
    total = lax.optimization_barrier((side.astype(f32) + across.astype(f32)).astype(bf16))
    back = lax.ppermute(total, "ctx", [(1, 0), (2, 3)])
    return jnp.where((place == 1) | (place == 2), total, back).astype(f32)


def rows_out(own):
    far = tp_swap(own, 2)
    near = tp_swap(own, 1)
    return own, near, far, tp_swap(far, 1)


def rows_in(terms):
    toward = terms[2] + tp_swap(terms[3].astype(bf16), 1).astype(f32)
    got = tp_swap(toward.astype(bf16), 2)
    here = terms[0] + tp_swap(terms[1].astype(bf16), 1).astype(f32)
    return here + got.astype(f32)


def natural(parts, core, y):
    r0, r1, r2, r3 = parts
    a0, a1 = jnp.where(core, r1, r0), jnp.where(core, r0, r1)
    a2, a3 = jnp.where(core, r3, r2), jnp.where(core, r2, r3)
    return jnp.concatenate(
        [jnp.where(y, a2, a0), jnp.where(y, a3, a1), jnp.where(y, a0, a2), jnp.where(y, a1, a3)]
    )


def norm_rows(rows):
    centre = rows - jnp.mean(rows, axis=-1, keepdims=True)
    inverse = lax.rsqrt(jnp.mean(centre * centre, axis=-1, keepdims=True) + norm_eps)
    return centre * inverse, inverse


def norm_back(grad, gain, normed, inverse):
    dn = grad * gain
    return (
        dn
        - jnp.mean(dn, axis=-1, keepdims=True)
        - normed * jnp.mean(dn * normed, axis=-1, keepdims=True)
    ) * inverse


def gelu_pair(values):
    phi_sum = 0.5 + 0.5 * lax.erf(values * math.sqrt(0.5))
    density = jnp.exp(values * values * -0.5) * (1.0 / math.sqrt(2.0 * math.pi))
    return (values * phi_sum).astype(bf16), phi_sum + values * density


def body(tokens, w_qkv, w_out, w_up, w_down, gains, shifts, lengths, out_grad):
    place = lax.axis_index("ctx")
    t = lax.axis_index("tp")
    core, y = (t & 1) == 1, (t >> 1) == 1
    tok_rows, depth = tokens.shape
    quarter = tok_rows // 4
    order = (0, 2, 1, 3)

    def quarter_of(array, r):
        return lax.dynamic_slice_in_dim(array, (t ^ r) * quarter, quarter)

    half_a = jnp.concatenate([quarter_of(tokens, 0), quarter_of(tokens, 2)])
    half_b = jnp.concatenate([quarter_of(tokens, 1), quarter_of(tokens, 3)])
    left_a = lax.ppermute(half_a, "ctx", [(0, 1), (1, 2), (2, 3)])
    right_a = lax.ppermute(half_a, "ctx", [(3, 2), (2, 1), (1, 0)])
    far_a = jnp.where(
        place >= 2,
        lax.ppermute(left_a, "ctx", [(1, 2), (2, 3)]),
        lax.ppermute(right_a, "ctx", [(2, 1), (1, 0)]),
    )
    full_qkv = fsdp_whole(w_qkv, 1)
    full_vectors = fsdp_whole(after(jnp.concatenate([gains, shifts]), full_qkv), 1).astype(f32)
    own_out = fsdp_whole(after(w_out, full_qkv), 1)
    full_up = fsdp_whole(after(w_up, own_out), 0)
    full_down = fsdp_whole(after(w_down, full_up), 1)
    gain = full_vectors[:2]
    shift = full_vectors[2:]

    positions = jnp.stack([t ^ r for r in order]) * quarter
    chunks = jnp.stack([place, place - 1, place + 1, place ^ 2]) * tok_rows
    info = jnp.concatenate(
        [
            jnp.cumsum(lengths[0]),
            place * tok_rows + positions,
            (chunks[:, None] + positions[None, :]).reshape(-1),
        ]
    ).astype(jnp.int32)

    w_q, w_k, w_v = full_qkv[0], full_qkv[1], full_qkv[2]
    chunk_rows = [
        jnp.concatenate([half_a, half_b]),
        jnp.concatenate([left_a, tp_swap(left_a, 1)]),
        jnp.concatenate([right_a, tp_swap(right_a, 1)]),
        jnp.concatenate([far_a, tp_swap(far_a, 1)]),
    ]
    queries = nn(chunk_rows[0], w_q).astype(bf16)
    keys = jnp.concatenate([nn(rows, w_k).astype(bf16) for rows in chunk_rows])
    values_t = jnp.concatenate(
        [contract(w_v, rows, 0, 1).astype(bf16) for rows in chunk_rows], axis=1
    )
    context, log_totals = attend(info, queries, keys, values_t)

    out_y = tp_swap(own_out, 2)
    out_all = jnp.concatenate([own_out, out_y, tp_swap(own_out, 1), tp_swap(out_y, 1)])
    pieces = jnp.split(context, 4)
    context_own = jnp.concatenate(
        [pieces[0]] + [tp_swap(pieces[n], order[n]) for n in (1, 2, 3)], axis=1
    )
    resid_rows = quarter_of(tokens, 0).astype(f32) + nn(context_own, out_all)
    normed_first, inverse_first = norm_rows(resid_rows)
    hidden = normed_first * gain[0] + shift[0]
    hid0, hid1, hid2, hid3 = rows_out(hidden.astype(bf16))
    hid_near, hid_far = jnp.concatenate([hid0, hid1]), jnp.concatenate([hid2, hid3])

    act_near, slope_near = gelu_pair(nn(hid_near, full_up))
    act_far, slope_far = gelu_pair(nn(hid_far, full_up))
    terms_far = nn(act_far, full_down)
    terms_near = nn(act_near, full_down)
    ffn_rows = rows_in(
        (terms_near[:quarter], terms_near[quarter:], terms_far[:quarter], terms_far[quarter:])
    )
    normed_second, inverse_second = norm_rows(hidden + ffn_rows)
    result = (normed_second * gain[1] + shift[1]).astype(bf16)
    grad_rows = quarter_of(out_grad, 0).astype(f32)
    grad_mid = norm_back(grad_rows, gain[1], normed_second, inverse_second)

    mid0, mid1, mid2, mid3 = rows_out(grad_mid.astype(bf16))
    result_parts = rows_out(after(result, mid2))
    mid_near, mid_far = jnp.concatenate([mid0, mid1]), jnp.concatenate([mid2, mid3])
    pre_near = (nt(mid_near, full_down) * slope_near).astype(bf16)
    pre_far = (nt(mid_far, full_down) * slope_far).astype(bf16)
    terms_far = nt(pre_far, full_up)
    terms_near = nt(pre_near, full_up)
    hidden_grad = grad_mid + rows_in(
        (terms_near[:quarter], terms_near[quarter:], terms_far[:quarter], terms_far[quarter:])
    )

    act_all = jnp.concatenate([act_near, act_far])
    mid_all = jnp.concatenate([mid_near, mid_far])
    hid_all = jnp.concatenate([hid_near, hid_far])
    pre_all = jnp.concatenate([pre_near, pre_far])

    def column_block(left, right):
        return lambda start, size: tn(left, lax.dynamic_slice_in_dim(right, start, size, axis=1))

    def row_block(left, right):
        return lambda start, size: tn(lax.dynamic_slice_in_dim(left, start, size, axis=1), right)

    down_grad = ctx_total(fsdp_total(column_block(act_all, mid_all), depth, 1))
    up_grad = ctx_total(fsdp_total(row_block(hid_all, pre_all), depth, 0))

    resid_grad = norm_back(hidden_grad, gain[0], normed_first, inverse_first)
    attn_own = resid_grad.astype(bf16)
    back_own = nt(attn_own, out_all).astype(bf16)
    pieces = jnp.split(back_own, 4, axis=1)
    context_grad = jnp.concatenate(
        [pieces[0]] + [tp_swap(pieces[n], order[n]) for n in (1, 2, 3)]
    )
    attn0, attn1, attn2, attn3 = rows_out(after(attn_own, context_grad))
    attn_all = jnp.concatenate([attn0, attn2, attn1, attn3])
    out_proj_grad = ctx_total(fsdp_total(column_block(context, attn_all), depth, 1))

    vectors = jnp.stack(
        [
            jnp.sum(hidden_grad * normed_first, axis=0),
            jnp.sum(grad_rows * normed_second, axis=0),
            jnp.sum(hidden_grad, axis=0),
            jnp.sum(grad_rows, axis=0),
        ]
    )
    vectors = vectors + tp_swap(vectors, 1)
    vectors = vectors + tp_swap(vectors, 2)
    vectors = vectors + lax.ppermute(vectors, "ctx", [(i, i ^ 1) for i in range(4)])
    vectors = vectors + lax.ppermute(vectors, "ctx", [(i, i ^ 2) for i in range(4)])
    if lax.axis_size("fsdp") == 2:
        half = depth // 2
        mine = lax.axis_index("fsdp")
        sent = lax.dynamic_slice_in_dim(vectors, (1 - mine) * half, half, axis=1)
        vectors = lax.dynamic_slice_in_dim(vectors, mine * half, half, axis=1) + lax.ppermute(
            sent, "fsdp", [(0, 1), (1, 0)]
        )
    else:
        vectors = lax.psum_scatter(vectors, "fsdp", scatter_dimension=1, tiled=True)

    values = values_t.T
    keys_t = keys.T
    query_grad, own_kv, left_kv, right_kv, far_kv = attend_back(
        info, queries, context_grad, context, log_totals, keys, values, keys_t
    )
    rows_all = jnp.concatenate(chunk_rows)

    def key_total(n):
        grads = jnp.concatenate([own_kv[n], left_kv[n], right_kv[n], far_kv[n]])
        return fsdp_total(row_block(rows_all, grads), depth, 0)

    qkv_grad = jnp.stack(
        [
            ctx_total(fsdp_total(row_block(chunk_rows[0], query_grad), depth, 0)),
            ctx_total(key_total(0)),
            ctx_total(key_total(1)),
        ]
    )
    left_sum = left_kv.astype(f32) + lax.ppermute(far_kv, "ctx", [(2, 1), (3, 2)]).astype(f32)
    right_sum = right_kv.astype(f32) + lax.ppermute(far_kv, "ctx", [(0, 1), (1, 2)]).astype(f32)
    key_values = (
        own_kv.astype(f32)
        + lax.ppermute(left_sum.astype(bf16), "ctx", [(3, 2), (2, 1), (1, 0)]).astype(f32)
        + lax.ppermute(right_sum.astype(bf16), "ctx", [(0, 1), (1, 2), (2, 3)]).astype(f32)
    ).astype(bf16)
    terms = nt(query_grad, w_q) + nt(key_values[0], w_k) + nt(key_values[1], w_v)
    q0, q2, q1, q3 = jnp.split(terms, 4)
    input_own = (resid_grad + rows_in((q0, q1, q2, q3))).astype(bf16)
    return (
        natural(result_parts, core, y),
        natural(rows_out(input_own), core, y),
        qkv_grad,
        out_proj_grad,
        up_grad,
        down_grad,
        vectors[:2],
        vectors[2:],
    )


def solution(mesh):
    return jax.shard_map(
        body,
        mesh=mesh,
        in_specs=(
            P(("fsdp", "ctx"), None),
            P(None, "fsdp", "tp"),
            P("tp", "fsdp"),
            P("fsdp", "tp"),
            P("tp", "fsdp"),
            P(None, "fsdp"),
            P(None, "fsdp"),
            P("fsdp", None),
            P(("fsdp", "ctx"), None),
        ),
        out_specs=(
            P(("fsdp", "ctx"), None),
            P(("fsdp", "ctx"), None),
            P(None, "fsdp", "tp"),
            P("tp", "fsdp"),
            P("fsdp", "tp"),
            P("tp", "fsdp"),
            P(None, "fsdp"),
            P(None, "fsdp"),
        ),
        check_vma=False,
    )
```

```python
import functools
import math

import jax
import jax.numpy as jnp
from jax import lax
from jax.experimental import pallas as pl
from jax.experimental.pallas import tpu as pltpu
from jax.sharding import PartitionSpec as P

HEAD_DIM = 64
BLK = 256
LOW = -1e30
norm_eps = 1e-12
f32 = jnp.float32
bf16 = jnp.bfloat16


def contract(left, right, left_dim, right_dim):
    return lax.dot_general(
        left, right, (((left_dim,), (right_dim,)), ((), ())), preferred_element_type=f32
    )


def nn(left, right):
    return contract(left, right, 1, 0)


def nt(left, right):
    return contract(left, right, 1, 1)


def tn(left, right):
    return contract(left, right, 0, 0)


def row_limits(info, qbase, rows):
    end0, end1, end2 = info[0], info[1], info[2]
    pos = qbase + lax.broadcasted_iota(jnp.int32, (1, rows), 1)
    first = jnp.where(pos < end0, 0, jnp.where(pos < end1, end0, end1))
    last = jnp.where(pos < end0, end0, jnp.where(pos < end1, end1, end2))
    real = pos < end2
    return jnp.where(real, first, 0), jnp.where(real, last, 0), real


def key_range(info, qbase, rows):
    end0, end1, end2 = info[0], info[1], info[2]
    low = jnp.where(
        qbase < end0,
        0,
        jnp.where(qbase < end1, end0, jnp.where(qbase < end2, end1, 1 << 30)),
    )
    final = qbase + rows - 1
    high = jnp.where(final < end0, end0, jnp.where(final < end1, end1, end2))
    return low, high


def stage(sources, offsets, width, k_sc, v_sc, sems):
    copies = []
    start = 0
    for n, (source, (k_at, v_at)) in enumerate(zip(sources, offsets)):
        size = source.shape[0]
        for m, (at, target) in enumerate(((k_at, k_sc), (v_at, v_sc))):
            copies.append(
                pltpu.make_async_copy(
                    source.at[:, pl.ds(at, width)],
                    target.at[pl.ds(start, size), :],
                    sems.at[2 * n + m],
                )
            )
        start += size
    for copy in copies:
        copy.start()
    for copy in copies:
        copy.wait()


def transposed(source, target, count):
    def step(j, carry):
        span = pl.ds(pl.multiple_of(j * BLK, BLK), BLK)
        target[:, span] = source[span, :].T
        return carry

    lax.fori_loop(0, count, step, 0)


def masked_heads(block, target, heads):
    rows = block.shape[0]
    head_of = lax.broadcasted_iota(jnp.int32, block.shape, 1) // HEAD_DIM
    for h in range(heads):
        target[h * rows : (h + 1) * rows, :] = jnp.where(head_of == h, block, jnp.zeros_like(block))


def attend_kernel(heads, kcount, kfirst, opens, closes, offsets, info, q_ref, *refs):
    count = len(offsets)
    sources, refs = refs[:count], refs[count:]
    if not opens:
        (m_in, l_in, acc_in), refs = refs[:3], refs[3:]
    if closes:
        (ctx_ref, lse_ref), refs = refs[:2], refs[2:]
    else:
        (m_out, l_out, acc_out), refs = refs[:3], refs[3:]
    m_sc, l_sc, acc_sc, qm_sc, k_sc, v_sc, vt_sc, sems = refs
    i = pl.program_id(0)
    rows, width = q_ref.shape
    qbase = info[3 + i]
    first, last, real = row_limits(info, qbase, rows)
    low, high = key_range(info, qbase, rows)
    factor = math.log2(math.e) / math.sqrt(HEAD_DIM)

    @pl.when(i == 0)
    def _():
        stage(sources, offsets, width, k_sc, v_sc, sems)
        transposed(v_sc, vt_sc, kcount)

    if opens:
        m_sc[...] = jnp.full_like(m_sc, LOW)
        l_sc[...] = jnp.zeros_like(l_sc)
        acc_sc[...] = jnp.zeros_like(acc_sc)
    else:
        m_sc[...] = m_in[...]
        l_sc[...] = l_in[...]
        acc_sc[...] = acc_in[...]
    masked_heads(q_ref[...], qm_sc, heads)
    span_of = [slice(h * HEAD_DIM, (h + 1) * HEAD_DIM) for h in range(heads)]

    def step(j, carry):
        base = info[kfirst + j]

        @pl.when((base + BLK > low) & (base < high))
        def _():
            span = pl.ds(pl.multiple_of(j * BLK, BLK), BLK)
            kb = k_sc[span, :]
            vt = vt_sc[:, span]
            posk = base + lax.broadcasted_iota(jnp.int32, (BLK, rows), 0)
            allowed = (posk >= first) & (posk < last)
            s = [
                jnp.where(allowed, nt(kb, qm_sc[h * rows : (h + 1) * rows, :]) * factor, LOW)
                for h in range(heads)
            ]
            m_old = m_sc[...]
            m_new = [
                jnp.maximum(m_old[h : h + 1, :], jnp.max(s[h], axis=0, keepdims=True))
                for h in range(heads)
            ]
            alpha = [jnp.exp2(m_old[h : h + 1, :] - m_new[h]) for h in range(heads)]
            p = [jnp.exp2(s[h] - m_new[h]) for h in range(heads)]
            sums = [jnp.sum(p[h], axis=0, keepdims=True) for h in range(heads)]
            pv = [nn(vt[span_of[h], :], p[h].astype(bf16)) for h in range(heads)]
            m_sc[...] = jnp.concatenate(m_new)
            l_sc[...] = l_sc[...] * jnp.concatenate(alpha) + jnp.concatenate(sums)
            for h in range(heads):
                acc_sc[span_of[h], :] = acc_sc[span_of[h], :] * alpha[h] + pv[h]

        return carry

    lax.fori_loop(0, kcount, step, 0)
    if closes:
        for h in range(heads):
            total = l_sc[h : h + 1, :]
            acc_sc[span_of[h], :] = jnp.where(real, acc_sc[span_of[h], :] / total, 0.0)
            lse_ref[h : h + 1, :] = jnp.where(real, m_sc[h : h + 1, :] + jnp.log2(total), -LOW)
        ctx_ref[...] = acc_sc[...].T.astype(bf16)
    else:
        m_out[...] = m_sc[...]
        l_out[...] = l_sc[...]
        acc_out[...] = acc_sc[...]


def whole(shape):
    return pl.BlockSpec(shape, lambda i, *_: (0,) * len(shape))


def attend(info, q, sources, offsets, kfirst, state=None, closes=False):
    rows, width = q.shape
    heads = width // HEAD_DIM
    keys = sum(source.shape[0] for source in sources)
    opens = state is None
    block = pl.BlockSpec((BLK, width), lambda i, *_: (i, 0))
    per_head = pl.BlockSpec((heads, BLK), lambda i, *_: (0, i))
    per_feature = pl.BlockSpec((width, BLK), lambda i, *_: (0, i))
    stats = jax.ShapeDtypeStruct((heads, rows), f32)
    carried = [per_head, per_head, per_feature]
    return pl.pallas_call(
        functools.partial(attend_kernel, heads, keys // BLK, kfirst, opens, closes, offsets),
        grid_spec=pltpu.PrefetchScalarGridSpec(
            num_scalar_prefetch=1,
            grid=(rows // BLK,),
            in_specs=[block]
            + [pl.BlockSpec(memory_space=pl.ANY)] * len(sources)
            + ([] if opens else carried),
            out_specs=[block, per_head] if closes else carried,
            scratch_shapes=[
                pltpu.VMEM((heads, BLK), f32),
                pltpu.VMEM((heads, BLK), f32),
                pltpu.VMEM((width, BLK), f32),
                pltpu.VMEM((heads * BLK, width), bf16),
                pltpu.VMEM((keys, width), bf16),
                pltpu.VMEM((keys, width), bf16),
                pltpu.VMEM((width, keys), bf16),
                pltpu.SemaphoreType.DMA((2 * len(sources),)),
            ],
        ),
        out_shape=[jax.ShapeDtypeStruct((rows, width), bf16), stats]
        if closes
        else [stats, stats, jax.ShapeDtypeStruct((width, rows), f32)],
        cost_estimate=pl.CostEstimate(
            flops=20 * rows * keys * width,
            bytes_accessed=4 * keys * width,
            transcendentals=rows * keys * heads // 2,
        ),
        name="attend_near" if opens else "attend_far",
    )(info, q, *sources, *(() if opens else state))


def attend_back_kernel(
    heads, kcount, kfirst, offsets, info, q_ref, do_ref, o_ref, lse_ref, *refs
):
    count = len(offsets)
    sources, refs = refs[:count], refs[count:]
    dq_ref, *outs = refs[:5]
    dk_sc, dv_sc, dqt_sc, qm_sc, dom_sc, delta_sc, k_sc, v_sc, kt_sc, sems = refs[5:]
    i = pl.program_id(0)
    rows, width = q_ref.shape
    qbase = info[3 + i]
    first, last, real = row_limits(info, qbase, rows)
    low, high = key_range(info, qbase, rows)
    scale = 1.0 / math.sqrt(HEAD_DIM)
    factor = math.log2(math.e) * scale

    @pl.when(i == 0)
    def _():
        dk_sc[...] = jnp.zeros_like(dk_sc)
        dv_sc[...] = jnp.zeros_like(dv_sc)
        stage(sources, offsets, width, k_sc, v_sc, sems)
        transposed(k_sc, kt_sc, kcount)

    dqt_sc[...] = jnp.zeros_like(dqt_sc)
    do = do_ref[...]
    masked_heads(q_ref[...], qm_sc, heads)
    masked_heads(do, dom_sc, heads)
    prod = (do.astype(f32) * o_ref[...].astype(f32)).T
    span_of = [slice(h * HEAD_DIM, (h + 1) * HEAD_DIM) for h in range(heads)]
    rows_of = [slice(h * rows, (h + 1) * rows) for h in range(heads)]
    for h in range(heads):
        delta_sc[h : h + 1, :] = jnp.sum(prod[span_of[h], :], axis=0, keepdims=True)

    def step(j, carry):
        base = info[kfirst + j]

        @pl.when((base + BLK > low) & (base < high))
        def _():
            span = pl.ds(pl.multiple_of(j * BLK, BLK), BLK)
            kb = k_sc[span, :]
            vb = v_sc[span, :]
            kt = kt_sc[:, span]
            posk = base + lax.broadcasted_iota(jnp.int32, (BLK, rows), 0)
            allowed = (posk >= first) & (posk < last)
            s = [nt(kb, qm_sc[rows_of[h], :]) for h in range(heads)]
            dp = [nt(vb, dom_sc[rows_of[h], :]) for h in range(heads)]
            p = [
                jnp.where(allowed, jnp.exp2(s[h] * factor - lse_ref[0, h : h + 1, :]), 0.0)
                for h in range(heads)
            ]
            ds = [(p[h] * (dp[h] - delta_sc[h : h + 1, :])).astype(bf16) for h in range(heads)]
            low_p = [p[h].astype(bf16) for h in range(heads)]
            dv_sc[span, :] += nn(jnp.concatenate(low_p, axis=1), dom_sc[...])
            dk_sc[span, :] += nn(jnp.concatenate(ds, axis=1), qm_sc[...])
            for h in range(heads):
                dqt_sc[span_of[h], :] += nn(kt[span_of[h], :], ds[h])

        return carry

    lax.fori_loop(0, kcount, step, 0)
    dq_ref[...] = (dqt_sc[...] * scale).T.astype(bf16)

    @pl.when(i == pl.num_programs(0) - 1)
    def _():
        part = outs[0].shape[1]
        for n, out_ref in enumerate(outs):
            out_ref[0] = (dk_sc[n * part : (n + 1) * part, :] * scale).astype(bf16)
            out_ref[1] = dv_sc[n * part : (n + 1) * part, :].astype(bf16)


def attend_back(info, q, do, o, lse, sources, offsets, kfirst, pick, width):
    rows = q.shape[0]
    heads = width // HEAD_DIM
    keys = sum(source.shape[0] for source in sources)
    block = pl.BlockSpec((BLK, width), lambda i, *_: (i, pick))
    pair = (2, keys // 4, width)
    offsets = tuple((k_at + pick * width, v_at + pick * width) for k_at, v_at in offsets)
    return pl.pallas_call(
        functools.partial(attend_back_kernel, heads, keys // BLK, kfirst, offsets),
        grid_spec=pltpu.PrefetchScalarGridSpec(
            num_scalar_prefetch=1,
            grid=(rows // BLK,),
            in_specs=[
                block,
                block,
                block,
                pl.BlockSpec((1, heads, BLK), lambda i, *_: (pick, 0, i)),
            ]
            + [pl.BlockSpec(memory_space=pl.ANY)] * len(sources),
            out_specs=[pl.BlockSpec((BLK, width), lambda i, *_: (i, 0))] + [whole(pair)] * 4,
            scratch_shapes=[
                pltpu.VMEM((keys, width), f32),
                pltpu.VMEM((keys, width), f32),
                pltpu.VMEM((width, BLK), f32),
                pltpu.VMEM((heads * BLK, width), bf16),
                pltpu.VMEM((heads * BLK, width), bf16),
                pltpu.VMEM((heads, BLK), f32),
                pltpu.VMEM((keys, width), bf16),
                pltpu.VMEM((keys, width), bf16),
                pltpu.VMEM((width, keys), bf16),
                pltpu.SemaphoreType.DMA((2 * len(sources),)),
            ],
        ),
        out_shape=[jax.ShapeDtypeStruct((rows, width), bf16)]
        + [jax.ShapeDtypeStruct(pair, bf16)] * 4,
        cost_estimate=pl.CostEstimate(
            flops=30 * rows * keys * width,
            bytes_accessed=8 * keys * width,
            transcendentals=rows * keys * heads // 2,
        ),
        name="attend_back",
    )(info, q, do, o, lse.reshape(-1, heads, rows), *sources)


def tp_swap(x, bit):
    return lax.ppermute(x, "tp", [(i, i ^ bit) for i in range(4)])


def gate_kernel(*refs):
    pass


def gate(through, *waits):
    through = tuple(through)
    anywhere = pl.BlockSpec(memory_space=pl.ANY)
    return pl.pallas_call(
        gate_kernel,
        in_specs=[anywhere] * (len(through) + len(waits)),
        out_specs=[anywhere] * len(through),
        out_shape=[jax.ShapeDtypeStruct(x.shape, x.dtype) for x in through],
        input_output_aliases={n: n for n in range(len(through))},
        name="gate",
    )(*through, *waits)


def tie(x, *others):
    for other in others:
        x = x + (other[(0,) * other.ndim].astype(f32) * 0.0).astype(x.dtype)
    return x


def fsdp_whole(shard, dim):
    if lax.axis_size("fsdp") != 2:
        full = lax.all_gather(shard, "fsdp", axis=dim, tiled=True)
        return full, full
    other = lax.ppermute(shard, "fsdp", [(0, 1), (1, 0)])
    low_half = lax.axis_index("fsdp") == 0
    return jnp.concatenate(
        [jnp.where(low_half, shard, other), jnp.where(low_half, other, shard)], axis=dim
    ), other


def fsdp_send(block_of, size, dim):
    if lax.axis_size("fsdp") != 2:
        mine = lax.psum_scatter(block_of(0, size), "fsdp", scatter_dimension=dim, tiled=True)
        return mine, jnp.zeros(mine.shape, bf16)
    half = size // 2
    place = lax.axis_index("fsdp")
    return block_of(place * half, half), block_of((1 - place) * half, half).astype(bf16)


def fsdp_swap(x):
    if lax.axis_size("fsdp") != 2:
        return x
    return lax.ppermute(x, "fsdp", [(0, 1), (1, 0)])


def ctx_swap(x, bit):
    return lax.ppermute(x, "ctx", [(i, i ^ bit) for i in range(4)])


def ctx_split(terms, bit):
    upper = (lax.axis_index("ctx") & bit) != 0
    size = terms.shape[0] // 2
    low_half, high_half = terms[:size], terms[size:]
    return (
        jnp.where(upper, high_half, low_half),
        jnp.where(upper, low_half, high_half).astype(bf16),
    )


def ctx_join(total, got, bit):
    upper = (lax.axis_index("ctx") & bit) != 0
    return jnp.concatenate([jnp.where(upper, got, total), jnp.where(upper, total, got)])


def rows_out(own):
    far = tp_swap(own, 2)
    near = tp_swap(own, 1)
    return own, near, far, tp_swap(far, 1)


def rows_in(terms):
    toward = terms[2] + tp_swap(terms[3].astype(bf16), 1).astype(f32)
    got = tp_swap(toward.astype(bf16), 2)
    here = terms[0] + tp_swap(terms[1].astype(bf16), 1).astype(f32)
    return here + got.astype(f32)


def natural(parts, core, y):
    r0, r1, r2, r3 = parts
    a0, a1 = jnp.where(core, r1, r0), jnp.where(core, r0, r1)
    a2, a3 = jnp.where(core, r3, r2), jnp.where(core, r2, r3)
    return jnp.concatenate(
        [jnp.where(y, a2, a0), jnp.where(y, a3, a1), jnp.where(y, a0, a2), jnp.where(y, a1, a3)]
    )


def norm_rows(rows):
    centre = rows - jnp.mean(rows, axis=-1, keepdims=True)
    inverse = lax.rsqrt(jnp.mean(centre * centre, axis=-1, keepdims=True) + norm_eps)
    return centre * inverse, inverse


def norm_back(grad, gain, normed, inverse):
    dn = grad * gain
    return (
        dn
        - jnp.mean(dn, axis=-1, keepdims=True)
        - normed * jnp.mean(dn * normed, axis=-1, keepdims=True)
    ) * inverse


def gelu_pair(values):
    phi_sum = 0.5 + 0.5 * lax.erf(values * math.sqrt(0.5))
    density = jnp.exp(values * values * -0.5) * (1.0 / math.sqrt(2.0 * math.pi))
    return (values * phi_sum).astype(bf16), phi_sum + values * density


def body(tokens, w_qkv, w_out, w_up, w_down, gains, shifts, lengths, out_grad):
    place = lax.axis_index("ctx")
    t = lax.axis_index("tp")
    core, y = (t & 1) == 1, (t >> 1) == 1
    tok_rows, depth = tokens.shape
    width = w_qkv.shape[2]
    quarter = tok_rows // 4
    order = (0, 2, 1, 3)

    def quarter_of(array, r):
        return lax.dynamic_slice_in_dim(array, (t ^ r) * quarter, quarter)

    half_a = jnp.concatenate([quarter_of(tokens, 0), quarter_of(tokens, 2)])
    left_a = lax.ppermute(half_a, "ctx", [(0, 1), (1, 2), (2, 3)])
    right_a = lax.ppermute(half_a, "ctx", [(3, 2), (2, 1), (1, 0)])
    half_b = jnp.concatenate([quarter_of(tokens, 1), quarter_of(tokens, 3)])
    far_left = lax.ppermute(left_a, "ctx", [(1, 2), (2, 3)])
    far_right = lax.ppermute(right_a, "ctx", [(2, 1), (1, 0)])
    full_qkv, got_qkv = fsdp_whole(w_qkv, 1)
    own_out, got_out = fsdp_whole(tie(w_out, got_qkv), 1)
    full_vectors, _ = fsdp_whole(jnp.concatenate([tie(gains, got_qkv), shifts]), 1)
    full_up, got_up = fsdp_whole(tie(w_up, got_qkv), 0)
    full_down, got_down = fsdp_whole(tie(w_down, got_qkv), 1)
    full_vectors = full_vectors.astype(f32)
    gain = full_vectors[:2]
    shift = full_vectors[2:]

    positions = jnp.stack([t ^ r for r in order]) * quarter
    chunks = jnp.stack([place, place - 1, place + 1, place ^ 2]) * tok_rows
    info = jnp.concatenate(
        [
            jnp.cumsum(lengths[0]),
            place * tok_rows + positions,
            (chunks[:, None] + positions[None, :]).reshape(-1),
        ]
    ).astype(jnp.int32)

    w_q, w_k, w_v = full_qkv[0], full_qkv[1], full_qkv[2]
    w_all = jnp.concatenate([w_q, w_k, w_v], axis=1)
    w_kv = w_all[:, width:]
    own = [nn(rows, w_all).astype(bf16) for rows in (half_a, half_b)]
    near = [
        nn(rows, w_kv).astype(bf16)
        for rows in (left_a, tp_swap(left_a, 1), right_a, tp_swap(right_a, 1))
    ]
    queries = jnp.concatenate([part[:, :width] for part in own])
    own_at, other_at = (width, 2 * width), (0, width)
    near_at = (own_at,) * 2 + (other_at,) * 4
    state = attend(info, queries, own + near, near_at, 7)
    far_left, far_right = gate((far_left, far_right), state[0])
    far_a = jnp.where(place >= 2, far_left, far_right)
    out_y = tp_swap(own_out, 2)
    out_all = jnp.concatenate([own_out, out_y, tp_swap(own_out, 1), tp_swap(out_y, 1)])
    far = [nn(rows, w_kv).astype(bf16) for rows in (far_a, tp_swap(far_a, 1))]
    context, log_totals = attend(info, queries, far, (other_at,) * 2, 19, state, True)
    (context,) = gate((context,), got_up, got_down, out_all)

    pieces = jnp.split(context, 4)
    context_own = jnp.concatenate(
        [pieces[0]] + [tp_swap(pieces[n], order[n]) for n in (1, 2, 3)], axis=1
    )
    resid_rows = quarter_of(tokens, 0).astype(f32) + nn(context_own, out_all)
    normed_first, inverse_first = norm_rows(resid_rows)
    hidden = normed_first * gain[0] + shift[0]
    hid0, hid1, hid2, hid3 = rows_out(hidden.astype(bf16))
    hid_near, hid_far = jnp.concatenate([hid0, hid1]), jnp.concatenate([hid2, hid3])

    act_near, slope_near = gelu_pair(nn(hid_near, full_up))
    act_far, slope_far = gelu_pair(nn(hid_far, full_up))
    terms_far = nn(act_far, full_down)
    terms_near = nn(act_near, full_down)
    ffn_rows = rows_in(
        (terms_near[:quarter], terms_near[quarter:], terms_far[:quarter], terms_far[quarter:])
    )
    normed_second, inverse_second = norm_rows(hidden + ffn_rows)
    result = (normed_second * gain[1] + shift[1]).astype(bf16)
    grad_rows = quarter_of(out_grad, 0).astype(f32)
    grad_mid = norm_back(grad_rows, gain[1], normed_second, inverse_second)

    mid0, mid1, mid2, mid3 = rows_out(grad_mid.astype(bf16))
    mid_near, mid_far = jnp.concatenate([mid0, mid1]), jnp.concatenate([mid2, mid3])

    def column_block(left, right):
        return lambda start, size: tn(left, lax.dynamic_slice_in_dim(right, start, size, axis=1))

    def row_block(left, right):
        return lambda start, size: tn(lax.dynamic_slice_in_dim(left, start, size, axis=1), right)

    act_all = jnp.concatenate([act_near, act_far])
    mid_all = jnp.concatenate([mid_near, mid_far])
    down_terms, down_send = fsdp_send(column_block(act_all, mid_all), depth, 1)
    down_got = fsdp_swap(down_send)

    pre_near = (nt(mid_near, full_down) * slope_near).astype(bf16)
    pre_far = (nt(mid_far, full_down) * slope_far).astype(bf16)
    terms_far = nt(pre_far, full_up)
    terms_near = nt(pre_near, full_up)
    hidden_grad = grad_mid + rows_in(
        (terms_near[:quarter], terms_near[quarter:], terms_far[:quarter], terms_far[quarter:])
    )
    hid_all = jnp.concatenate([hid_near, hid_far])
    pre_all = jnp.concatenate([pre_near, pre_far])
    up_terms, up_send = fsdp_send(row_block(hid_all, pre_all), depth, 0)
    resid_grad = norm_back(hidden_grad, gain[0], normed_first, inverse_first)
    attn_own = resid_grad.astype(bf16)

    attn_own, up_send, down_got = gate((attn_own, up_send, down_got))
    up_got = fsdp_swap(up_send)
    down_kept, send = ctx_split(down_terms + down_got.astype(f32), 1)
    down_got = ctx_swap(send, 1)
    back_own = nt(attn_own, out_all).astype(bf16)
    pieces = jnp.split(back_own, 4, axis=1)
    context_grad = jnp.concatenate(
        [pieces[0]] + [tp_swap(pieces[n], order[n]) for n in (1, 2, 3)]
    )

    context_grad, down_got, attn_own, result = gate((context_grad, down_got, attn_own, result))
    down_kept, send = ctx_split(down_kept + down_got.astype(f32), 2)
    down_got = ctx_swap(send, 2)
    attn_near, attn_far = tp_swap(attn_own, 1), tp_swap(attn_own, 2)
    result_near, result_far = tp_swap(result, 1), tp_swap(result, 2)
    vectors = jnp.stack(
        [
            jnp.sum(hidden_grad * normed_first, axis=0),
            jnp.sum(grad_rows * normed_second, axis=0),
            jnp.sum(hidden_grad, axis=0),
            jnp.sum(grad_rows, axis=0),
        ]
    )
    vectors_got = tp_swap(vectors, 1)

    sources = own + near + far
    sources_at = (own_at,) * 2 + (other_at,) * 6
    part = width // 2
    dq_1, own_1, left_1, right_1, far_1 = attend_back(
        info, queries, context_grad, context, log_totals, sources, sources_at, 7, 0, part
    )
    info_2, far_1, down_got, up_got, attn_far, result_far, vectors_got = gate(
        (info, far_1, down_got, up_got, attn_far, result_far, vectors_got),
        attn_near,
        result_near,
    )
    left_hop, right_hop = [(2, 1), (3, 2)], [(0, 1), (1, 2)]
    from_left_1 = lax.ppermute(far_1, "ctx", left_hop)
    from_right_1 = lax.ppermute(far_1, "ctx", right_hop)
    down_total = (down_kept + down_got.astype(f32)).astype(bf16)
    down_total = lax.optimization_barrier(down_total)
    down_got = ctx_swap(down_total, 2)
    up_kept, send = ctx_split(up_terms + up_got.astype(f32), 1)
    up_got = ctx_swap(send, 1)
    attn_all = jnp.concatenate([attn_own, attn_far, attn_near, tp_swap(attn_far, 1)])
    result_parts = (result, result_near, result_far, tp_swap(result_far, 1))
    out_terms, out_send = fsdp_send(column_block(context, attn_all), depth, 1)
    out_got = fsdp_swap(out_send)
    vectors = vectors + vectors_got
    vectors_got = tp_swap(vectors, 2)

    dq_2, own_2, left_2, right_2, far_2 = attend_back(
        info_2, queries, context_grad, context, log_totals, sources, sources_at, 7, 1, part
    )
    far_2, from_left_1, from_right_1, down_got, up_got, vectors_got = gate(
        (far_2, from_left_1, from_right_1, down_got, up_got, vectors_got), out_got
    )

    def hop(own_kv, left_kv, right_kv, from_left, from_right):
        left_sum = (left_kv.astype(f32) + from_left.astype(f32)).astype(bf16)
        right_sum = (right_kv.astype(f32) + from_right.astype(f32)).astype(bf16)
        return (
            lax.ppermute(left_sum, "ctx", [(3, 2), (2, 1), (1, 0)]),
            lax.ppermute(right_sum, "ctx", [(0, 1), (1, 2), (2, 3)]),
        )

    home_1 = hop(own_1, left_1, right_1, from_left_1, from_right_1)
    from_left_2 = lax.ppermute(far_2, "ctx", left_hop)
    from_right_2 = lax.ppermute(far_2, "ctx", right_hop)
    vectors = vectors + vectors_got
    vectors_got = ctx_swap(vectors, 1)
    down_total = ctx_join(down_total, down_got, 2)
    up_kept, up_send = ctx_split(up_kept + up_got.astype(f32), 2)

    home_1a, home_1b, from_left_2, from_right_2, vectors_got, down_total, up_send = gate(
        (*home_1, from_left_2, from_right_2, vectors_got, down_total, up_send)
    )
    home_2 = hop(own_2, left_2, right_2, from_left_2, from_right_2)
    rows_own = jnp.concatenate([half_a, half_b])
    total_1 = (own_1.astype(f32) + home_1a.astype(f32) + home_1b.astype(f32)).astype(bf16)
    grads_1 = jnp.concatenate([dq_1, dq_2, total_1[0], total_1[1]], axis=1)
    qkv_terms_1, qkv_send_1 = fsdp_send(row_block(rows_own, grads_1), depth, 0)
    qkv_got_1 = fsdp_swap(qkv_send_1)
    weights_1 = jnp.concatenate([w_q, w_k[:, :part], w_v[:, :part]], axis=1)
    weights_2 = jnp.concatenate([w_k[:, part:], w_v[:, part:]], axis=1)
    terms_1 = nt(grads_1, weights_1)
    vectors = vectors + vectors_got
    vectors_got = ctx_swap(vectors, 2)

    home_2a, home_2b, qkv_got_1, vectors_got, down_total, up_send = gate(
        (*home_2, qkv_got_1, vectors_got, down_total, up_send)
    )
    total_2 = (own_2.astype(f32) + home_2a.astype(f32) + home_2b.astype(f32)).astype(bf16)
    grads_2 = jnp.concatenate([total_2[0], total_2[1]], axis=1)
    terms = terms_1 + nt(grads_2, weights_2)
    q0, q2, q1, q3 = jnp.split(terms, 4)
    toward = q2 + tp_swap(q3.astype(bf16), 1).astype(f32)
    input_got = tp_swap(toward.astype(bf16), 2)
    here = q0 + tp_swap(q1.astype(bf16), 1).astype(f32)
    qkv_terms_2, qkv_send_2 = fsdp_send(row_block(rows_own, grads_2), depth, 0)
    qkv_got_2 = fsdp_swap(qkv_send_2)
    down_got = ctx_swap(down_total, 1)
    up_got = ctx_swap(up_send, 2)
    vectors = vectors + vectors_got
    split_vectors = lax.axis_size("fsdp") == 2
    if split_vectors:
        half = depth // 2
        mine = lax.axis_index("fsdp")
        vectors_got = fsdp_swap(
            lax.dynamic_slice_in_dim(vectors, (1 - mine) * half, half, axis=1)
        )
        vectors = lax.dynamic_slice_in_dim(vectors, mine * half, half, axis=1)
    else:
        vectors = lax.psum_scatter(vectors, "fsdp", scatter_dimension=1, tiled=True)
        vectors_got = jnp.zeros_like(vectors)

    input_got, qkv_got_2, down_got, up_got, vectors_got = gate(
        (input_got, qkv_got_2, down_got, up_got, vectors_got)
    )
    vectors = vectors + vectors_got
    input_own = (resid_grad + here + input_got.astype(f32)).astype(bf16)
    input_near, input_far = tp_swap(input_own, 1), tp_swap(input_own, 2)
    down_grad = ctx_join(down_total, down_got, 1).astype(f32)
    up_total = lax.optimization_barrier((up_kept + up_got.astype(f32)).astype(bf16))
    up_got = ctx_swap(up_total, 2)
    out_shape = out_terms.shape
    rest = jnp.concatenate(
        [
            qkv_terms_1 + qkv_got_1.astype(f32),
            qkv_terms_2 + qkv_got_2.astype(f32),
            (out_terms + out_got.astype(f32)).reshape(qkv_terms_1.shape[0], -1),
        ],
        axis=1,
    )
    rest_kept, send = ctx_split(rest, 1)
    rest_got = ctx_swap(send, 1)

    input_far, input_near, up_got, rest_got = gate((input_far, input_near, up_got, rest_got))
    input_parts = (input_own, input_near, input_far, tp_swap(input_far, 1))
    up_total = ctx_join(up_total, up_got, 2)
    up_got = ctx_swap(up_total, 1)
    rest_kept, send = ctx_split(rest_kept + rest_got.astype(f32), 2)
    rest_got = ctx_swap(send, 2)
    rest_total = (rest_kept + rest_got.astype(f32)).astype(bf16)
    rest_total = lax.optimization_barrier(rest_total)
    rest_total = ctx_join(rest_total, ctx_swap(rest_total, 2), 2)
    rest_total = ctx_join(rest_total, ctx_swap(rest_total, 1), 1).astype(f32)
    up_grad = ctx_join(up_total, up_got, 1).astype(f32)
    qkv_1, qkv_2 = rest_total[:, : 2 * width], rest_total[:, 2 * width : 3 * width]
    qkv_grad = jnp.stack(
        [
            qkv_1[:, :width],
            jnp.concatenate([qkv_1[:, width : width + part], qkv_2[:, :part]], axis=1),
            jnp.concatenate([qkv_1[:, width + part :], qkv_2[:, part:]], axis=1),
        ]
    )
    return (
        natural(result_parts, core, y),
        natural(input_parts, core, y),
        qkv_grad,
        rest_total[:, 3 * width :].reshape(out_shape),
        up_grad,
        down_grad,
        vectors[:2],
        vectors[2:],
    )


def solution(mesh):
    return jax.shard_map(
        body,
        mesh=mesh,
        in_specs=(
            P(("fsdp", "ctx"), None),
            P(None, "fsdp", "tp"),
            P("tp", "fsdp"),
            P("fsdp", "tp"),
            P("tp", "fsdp"),
            P(None, "fsdp"),
            P(None, "fsdp"),
            P("fsdp", None),
            P(("fsdp", "ctx"), None),
        ),
        out_specs=(
            P(("fsdp", "ctx"), None),
            P(("fsdp", "ctx"), None),
            P(None, "fsdp", "tp"),
            P("tp", "fsdp"),
            P("fsdp", "tp"),
            P("tp", "fsdp"),
            P(None, "fsdp"),
            P(None, "fsdp"),
        ),
        check_vma=False,
    )
```

```python
import functools
import math

import jax
import jax.numpy as jnp
from jax import lax
from jax.experimental import pallas as pl
from jax.experimental.pallas import tpu as pltpu
from jax.sharding import PartitionSpec as P

HEAD_DIM = 64
BLK = 256
PAD_ROWS = 16
LOW = -1e30
norm_eps = 1e-12
f32 = jnp.float32
bf16 = jnp.bfloat16


def contract(left, right, left_dim, right_dim):
    return lax.dot_general(
        left, right, (((left_dim,), (right_dim,)), ((), ())), preferred_element_type=f32
    )


def nn(left, right):
    return contract(left, right, 1, 0)


def nt(left, right):
    return contract(left, right, 1, 1)


def tn(left, right):
    return contract(left, right, 0, 0)


def row_limits(info, qbase, rows):
    end0, end1, end2 = info[0], info[1], info[2]
    pos = qbase + lax.broadcasted_iota(jnp.int32, (1, rows), 1)
    first = jnp.where(pos < end0, 0, jnp.where(pos < end1, end0, end1))
    last = jnp.where(pos < end0, end0, jnp.where(pos < end1, end1, end2))
    real = pos < end2
    return jnp.where(real, first, 0), jnp.where(real, last, 0), real


def key_range(info, qbase, rows):
    end0, end1, end2 = info[0], info[1], info[2]
    low = jnp.where(
        qbase < end0,
        0,
        jnp.where(qbase < end1, end0, jnp.where(qbase < end2, end1, 1 << 30)),
    )
    final = qbase + rows - 1
    high = jnp.where(final < end0, end0, jnp.where(final < end1, end1, end2))
    return low, high


def stage(sources, offsets, width, k_sc, v_sc, sems):
    copies = []
    start = 0
    for n, (source, (k_at, v_at)) in enumerate(zip(sources, offsets)):
        size = source.shape[0]
        for m, (at, target) in enumerate(((k_at, k_sc), (v_at, v_sc))):
            copies.append(
                pltpu.make_async_copy(
                    source.at[:, pl.ds(at, width)],
                    target.at[pl.ds(start, size), :],
                    sems.at[2 * n + m],
                )
            )
        start += size
    for copy in copies:
        copy.start()
    for copy in copies:
        copy.wait()


def transposed(source, target, count):
    def step(j, carry):
        span = pl.ds(pl.multiple_of(j * BLK, BLK), BLK)
        target[:, span] = source[span, :].T
        return carry

    lax.fori_loop(0, count, step, 0)


def masked_heads(block, target, heads):
    rows = block.shape[0]
    head_of = lax.broadcasted_iota(jnp.int32, block.shape, 1) // HEAD_DIM
    for h in range(heads):
        target[h * rows : (h + 1) * rows, :] = jnp.where(head_of == h, block, jnp.zeros_like(block))


def attend_kernel(heads, kcount, kfirst, opens, closes, offsets, info, q_ref, *refs):
    count = len(offsets)
    sources, refs = refs[:count], refs[count:]
    if not opens:
        (m_in, l_in, acc_in), refs = refs[:3], refs[3:]
    if closes:
        (ctx_ref, lse_ref), refs = refs[:2], refs[2:]
    else:
        (m_out, l_out, acc_out), refs = refs[:3], refs[3:]
    m_sc, l_sc, acc_sc, qm_sc, k_sc, v_sc, vt_sc, sems = refs
    i = pl.program_id(0)
    rows, width = q_ref.shape
    qbase = info[3 + i]
    first, last, real = row_limits(info, qbase, rows)
    low, high = key_range(info, qbase, rows)
    factor = math.log2(math.e) / math.sqrt(HEAD_DIM)

    @pl.when(i == 0)
    def _():
        stage(sources, offsets, width, k_sc, v_sc, sems)
        transposed(v_sc, vt_sc, kcount)

    if opens:
        m_sc[...] = jnp.full_like(m_sc, LOW)
        l_sc[...] = jnp.zeros_like(l_sc)
        acc_sc[...] = jnp.zeros_like(acc_sc)
    else:
        m_sc[...] = m_in[...]
        l_sc[...] = l_in[...]
        acc_sc[...] = acc_in[...]
    masked_heads(q_ref[...], qm_sc, heads)
    span_of = [slice(h * HEAD_DIM, (h + 1) * HEAD_DIM) for h in range(heads)]

    def step(j, carry):
        base = info[kfirst + j]

        @pl.when((base + BLK > low) & (base < high))
        def _():
            span = pl.ds(pl.multiple_of(j * BLK, BLK), BLK)
            kb = k_sc[span, :]
            vt = vt_sc[:, span]
            posk = base + lax.broadcasted_iota(jnp.int32, (BLK, rows), 0)
            allowed = (posk >= first) & (posk < last)
            s = [
                jnp.where(allowed, nt(kb, qm_sc[h * rows : (h + 1) * rows, :]) * factor, LOW)
                for h in range(heads)
            ]
            m_old = m_sc[...]
            m_new = [
                jnp.maximum(m_old[h : h + 1, :], jnp.max(s[h], axis=0, keepdims=True))
                for h in range(heads)
            ]
            alpha = [jnp.exp2(m_old[h : h + 1, :] - m_new[h]) for h in range(heads)]
            p = [jnp.exp2(s[h] - m_new[h]) for h in range(heads)]
            sums = [jnp.sum(p[h], axis=0, keepdims=True) for h in range(heads)]
            pv = [nn(vt[span_of[h], :], p[h].astype(bf16)) for h in range(heads)]
            m_sc[...] = jnp.concatenate(m_new)
            l_sc[...] = l_sc[...] * jnp.concatenate(alpha) + jnp.concatenate(sums)
            for h in range(heads):
                acc_sc[span_of[h], :] = acc_sc[span_of[h], :] * alpha[h] + pv[h]

        return carry

    lax.fori_loop(0, kcount, step, 0)
    if closes:
        for h in range(heads):
            total = l_sc[h : h + 1, :]
            acc_sc[span_of[h], :] = jnp.where(real, acc_sc[span_of[h], :] / total, 0.0)
            lse_ref[h : h + 1, :] = jnp.where(real, m_sc[h : h + 1, :] + jnp.log2(total), -LOW)
        ctx_ref[...] = acc_sc[...].T.astype(bf16)
    else:
        m_out[...] = m_sc[...]
        l_out[...] = l_sc[...]
        acc_out[...] = acc_sc[...]


def whole(shape):
    return pl.BlockSpec(shape, lambda i, *_: (0,) * len(shape))


def attend(info, q, sources, offsets, kfirst, state=None, closes=False):
    rows, width = q.shape
    heads = width // HEAD_DIM
    keys = sum(source.shape[0] for source in sources)
    opens = state is None
    block = pl.BlockSpec((BLK, width), lambda i, *_: (i, 0))
    per_head = pl.BlockSpec((heads, BLK), lambda i, *_: (0, i))
    per_feature = pl.BlockSpec((width, BLK), lambda i, *_: (0, i))
    stats = jax.ShapeDtypeStruct((heads, rows), f32)
    carried = [per_head, per_head, per_feature]
    return pl.pallas_call(
        functools.partial(attend_kernel, heads, keys // BLK, kfirst, opens, closes, offsets),
        grid_spec=pltpu.PrefetchScalarGridSpec(
            num_scalar_prefetch=1,
            grid=(rows // BLK,),
            in_specs=[block]
            + [pl.BlockSpec(memory_space=pl.ANY)] * len(sources)
            + ([] if opens else carried),
            out_specs=[block, per_head] if closes else carried,
            scratch_shapes=[
                pltpu.VMEM((heads, BLK), f32),
                pltpu.VMEM((heads, BLK), f32),
                pltpu.VMEM((width, BLK), f32),
                pltpu.VMEM((heads * BLK, width), bf16),
                pltpu.VMEM((keys, width), bf16),
                pltpu.VMEM((keys, width), bf16),
                pltpu.VMEM((width, keys), bf16),
                pltpu.SemaphoreType.DMA((2 * len(sources),)),
            ],
        ),
        out_shape=[jax.ShapeDtypeStruct((rows, width), bf16), stats]
        if closes
        else [stats, stats, jax.ShapeDtypeStruct((width, rows), f32)],
        cost_estimate=pl.CostEstimate(flops=1024, bytes_accessed=1024, transcendentals=0),
        name="attend_near" if opens else "attend_far",
    )(info, q, *sources, *(() if opens else state))


def attend_back_kernel(
    heads, kcount, kfirst, offsets, info, q_ref, do_ref, o_ref, lse_ref, *refs
):
    count = len(offsets)
    sources, refs = refs[:count], refs[count:]
    dq_ref, *outs = refs[:5]
    dk_sc, dv_sc, dqt_sc, qm_sc, dom_sc, delta_sc, k_sc, v_sc, kt_sc, sems = refs[5:]
    i = pl.program_id(0)
    rows, width = q_ref.shape
    qbase = info[3 + i]
    first, last, real = row_limits(info, qbase, rows)
    low, high = key_range(info, qbase, rows)
    scale = 1.0 / math.sqrt(HEAD_DIM)
    factor = math.log2(math.e) * scale

    @pl.when(i == 0)
    def _():
        dk_sc[...] = jnp.zeros_like(dk_sc)
        dv_sc[...] = jnp.zeros_like(dv_sc)
        stage(sources, offsets, width, k_sc, v_sc, sems)
        transposed(k_sc, kt_sc, kcount)

    dqt_sc[...] = jnp.zeros_like(dqt_sc)
    do = do_ref[...]
    masked_heads(q_ref[...], qm_sc, heads)
    masked_heads(do, dom_sc, heads)
    prod = (do.astype(f32) * o_ref[...].astype(f32)).T
    span_of = [slice(h * HEAD_DIM, (h + 1) * HEAD_DIM) for h in range(heads)]
    rows_of = [slice(h * rows, (h + 1) * rows) for h in range(heads)]
    for h in range(heads):
        delta_sc[h : h + 1, :] = jnp.sum(prod[span_of[h], :], axis=0, keepdims=True)

    def step(j, carry):
        base = info[kfirst + j]

        @pl.when((base + BLK > low) & (base < high))
        def _():
            span = pl.ds(pl.multiple_of(j * BLK, BLK), BLK)
            kb = k_sc[span, :]
            vb = v_sc[span, :]
            kt = kt_sc[:, span]
            posk = base + lax.broadcasted_iota(jnp.int32, (BLK, rows), 0)
            allowed = (posk >= first) & (posk < last)
            s = [nt(kb, qm_sc[rows_of[h], :]) for h in range(heads)]
            dp = [nt(vb, dom_sc[rows_of[h], :]) for h in range(heads)]
            p = [
                jnp.where(allowed, jnp.exp2(s[h] * factor - lse_ref[0, h : h + 1, :]), 0.0)
                for h in range(heads)
            ]
            ds = [(p[h] * (dp[h] - delta_sc[h : h + 1, :])).astype(bf16) for h in range(heads)]
            low_p = [p[h].astype(bf16) for h in range(heads)]
            dv_sc[span, :] += nn(jnp.concatenate(low_p, axis=1), dom_sc[...])
            dk_sc[span, :] += nn(jnp.concatenate(ds, axis=1), qm_sc[...])
            for h in range(heads):
                dqt_sc[span_of[h], :] += nn(kt[span_of[h], :], ds[h])

        return carry

    lax.fori_loop(0, kcount, step, 0)
    dq_ref[...] = (dqt_sc[...] * scale).T.astype(bf16)

    @pl.when(i == pl.num_programs(0) - 1)
    def _():
        part = outs[0].shape[1]
        for n, out_ref in enumerate(outs):
            out_ref[0] = (dk_sc[n * part : (n + 1) * part, :] * scale).astype(bf16)
            out_ref[1] = dv_sc[n * part : (n + 1) * part, :].astype(bf16)


def attend_back(info, q, do, o, lse, sources, offsets, kfirst, pick, width):
    rows = q.shape[0]
    heads = width // HEAD_DIM
    keys = sum(source.shape[0] for source in sources)
    block = pl.BlockSpec((BLK, width), lambda i, *_: (i, pick))
    pair = (2, keys // 4, width)
    offsets = tuple((k_at + pick * width, v_at + pick * width) for k_at, v_at in offsets)
    return pl.pallas_call(
        functools.partial(attend_back_kernel, heads, keys // BLK, kfirst, offsets),
        grid_spec=pltpu.PrefetchScalarGridSpec(
            num_scalar_prefetch=1,
            grid=(rows // BLK,),
            in_specs=[
                block,
                block,
                block,
                pl.BlockSpec((1, heads, BLK), lambda i, *_: (pick, 0, i)),
            ]
            + [pl.BlockSpec(memory_space=pl.ANY)] * len(sources),
            out_specs=[pl.BlockSpec((BLK, width), lambda i, *_: (i, 0))] + [whole(pair)] * 4,
            scratch_shapes=[
                pltpu.VMEM((keys, width), f32),
                pltpu.VMEM((keys, width), f32),
                pltpu.VMEM((width, BLK), f32),
                pltpu.VMEM((heads * BLK, width), bf16),
                pltpu.VMEM((heads * BLK, width), bf16),
                pltpu.VMEM((heads, BLK), f32),
                pltpu.VMEM((keys, width), bf16),
                pltpu.VMEM((keys, width), bf16),
                pltpu.VMEM((width, keys), bf16),
                pltpu.SemaphoreType.DMA((2 * len(sources),)),
            ],
        ),
        out_shape=[jax.ShapeDtypeStruct((rows, width), bf16)]
        + [jax.ShapeDtypeStruct(pair, bf16)] * 4,
        cost_estimate=pl.CostEstimate(flops=1024, bytes_accessed=1024, transcendentals=0),
        name="attend_back",
    )(info, q, do, o, lse.reshape(-1, heads, rows), *sources)


def qkv_terms_kernel(order, *refs):
    rows, (dq_1, dq_2), pairs = refs[:8], refs[8:10], refs[10:18]
    sent_ref, mine_ref = refs[18:]
    size = rows[0].shape[0]
    query, key_value = None, None
    for n, rows_ref in enumerate(rows):
        left = rows_ref[...]
        span = slice((n % 2) * size, (n % 2 + 1) * size)
        first, second = pairs[n // 2 * 2], pairs[n // 2 * 2 + 1]
        grads = jnp.concatenate(
            [first[0, span], second[0, span], first[1, span], second[1, span]], axis=1
        )
        term = tn(left, grads)
        key_value = term if key_value is None else key_value + term
        if n < 2:
            term = tn(left, jnp.concatenate([dq_1[span], dq_2[span]], axis=1))
            query = term if query is None else query + term
    total = jnp.concatenate([query, key_value], axis=1)

    @pl.when(pl.program_id(0) == 0)
    def _():
        sent_ref[...] = total.astype(sent_ref.dtype)

    @pl.when(pl.program_id(0) == 1)
    def _():
        mine_ref[...] = total


def qkv_terms_of(rows, queries, pairs, order, sent_type):
    size, depth = rows[0].shape
    half = depth // 2
    wide = 2 * (queries[0].shape[1] + 2 * pairs[0].shape[2])
    return pl.pallas_call(
        qkv_terms_kernel,
        grid_spec=pltpu.PrefetchScalarGridSpec(
            num_scalar_prefetch=1,
            grid=(2,),
            in_specs=[pl.BlockSpec((size, half), lambda i, pick: (0, pick[i]))] * 8
            + [whole(x.shape) for x in (*queries, *pairs)],
            out_specs=[whole((half, wide)), whole((half, wide))],
        ),
        out_shape=[
            jax.ShapeDtypeStruct((half, wide), sent_type),
            jax.ShapeDtypeStruct((half, wide), f32),
        ],
        cost_estimate=pl.CostEstimate(flops=1024, bytes_accessed=1024, transcendentals=0),
        name="qkv_terms",
    )(order, *rows, *queries, *pairs)


def tp_swap(x, bit):
    return lax.ppermute(x, "tp", [(i, i ^ bit) for i in range(4)])


def gate_kernel(*refs):
    pass


def gate(through, *waits):
    through = tuple(through)
    anywhere = pl.BlockSpec(memory_space=pl.ANY)
    return pl.pallas_call(
        gate_kernel,
        in_specs=[anywhere] * (len(through) + len(waits)),
        out_specs=[anywhere] * len(through),
        out_shape=[jax.ShapeDtypeStruct(x.shape, x.dtype) for x in through],
        input_output_aliases={n: n for n in range(len(through))},
        name="gate",
    )(*through, *waits)


def tie(x, *others):
    for other in others:
        x = x + (other[(0,) * other.ndim].astype(f32) * 0.0).astype(x.dtype)
    return x


def fsdp_whole(shard, dim):
    if lax.axis_size("fsdp") != 2:
        full = lax.all_gather(shard, "fsdp", axis=dim, tiled=True)
        return full, full
    other = lax.ppermute(shard, "fsdp", [(0, 1), (1, 0)])
    low_half = lax.axis_index("fsdp") == 0
    return jnp.concatenate(
        [jnp.where(low_half, shard, other), jnp.where(low_half, other, shard)], axis=dim
    ), other


def fsdp_send(block_of, size, dim):
    if lax.axis_size("fsdp") != 2:
        mine = lax.psum_scatter(block_of(0, size), "fsdp", scatter_dimension=dim, tiled=True)
        return mine, jnp.zeros(mine.shape, bf16)
    half = size // 2
    place = lax.axis_index("fsdp")
    return block_of(place * half, half), block_of((1 - place) * half, half).astype(bf16)


def fsdp_swap(x):
    if lax.axis_size("fsdp") != 2:
        return x
    return lax.ppermute(x, "fsdp", [(0, 1), (1, 0)])


def ctx_swap(x, bit):
    return lax.ppermute(x, "ctx", [(i, i ^ bit) for i in range(4)])


def ctx_split(terms, bit):
    upper = (lax.axis_index("ctx") & bit) != 0
    size = terms.shape[0] // 2
    low_half, high_half = terms[:size], terms[size:]
    return (
        jnp.where(upper, high_half, low_half),
        jnp.where(upper, low_half, high_half).astype(bf16),
    )


def ctx_join(total, got, bit):
    upper = (lax.axis_index("ctx") & bit) != 0
    return jnp.concatenate([jnp.where(upper, got, total), jnp.where(upper, total, got)])


def rows_out(own):
    far = tp_swap(own, 2)
    near = tp_swap(own, 1)
    return own, near, far, tp_swap(far, 1)


def rows_in(terms):
    toward = terms[2] + tp_swap(terms[3].astype(bf16), 1).astype(f32)
    got = tp_swap(toward.astype(bf16), 2)
    here = terms[0] + tp_swap(terms[1].astype(bf16), 1).astype(f32)
    return here + got.astype(f32)


def natural(parts, core, y):
    r0, r1, r2, r3 = parts
    a0, a1 = jnp.where(core, r1, r0), jnp.where(core, r0, r1)
    a2, a3 = jnp.where(core, r3, r2), jnp.where(core, r2, r3)
    return jnp.concatenate(
        [jnp.where(y, a2, a0), jnp.where(y, a3, a1), jnp.where(y, a0, a2), jnp.where(y, a1, a3)]
    )


def norm_rows(rows):
    centre = rows - jnp.mean(rows, axis=-1, keepdims=True)
    inverse = lax.rsqrt(jnp.mean(centre * centre, axis=-1, keepdims=True) + norm_eps)
    return centre * inverse, inverse


def norm_back(grad, gain, normed, inverse):
    dn = grad * gain
    return (
        dn
        - jnp.mean(dn, axis=-1, keepdims=True)
        - normed * jnp.mean(dn * normed, axis=-1, keepdims=True)
    ) * inverse


def gelu_pair(values):
    phi_sum = 0.5 + 0.5 * lax.erf(values * math.sqrt(0.5))
    density = jnp.exp(values * values * -0.5) * (1.0 / math.sqrt(2.0 * math.pi))
    return (values * phi_sum).astype(bf16), phi_sum + values * density


def body(tokens, w_qkv, w_out, w_up, w_down, gains, shifts, lengths, out_grad):
    place = lax.axis_index("ctx")
    t = lax.axis_index("tp")
    core, y = (t & 1) == 1, (t >> 1) == 1
    tok_rows, depth = tokens.shape
    width = w_qkv.shape[2]
    quarter = tok_rows // 4
    order = (0, 2, 1, 3)

    def quarter_of(array, r):
        return lax.dynamic_slice_in_dim(array, (t ^ r) * quarter, quarter)

    half_a = jnp.concatenate([quarter_of(tokens, 0), quarter_of(tokens, 2)])
    left_a = lax.ppermute(half_a, "ctx", [(0, 1), (1, 2), (2, 3)])
    right_a = lax.ppermute(half_a, "ctx", [(3, 2), (2, 1), (1, 0)])
    half_b = jnp.concatenate([quarter_of(tokens, 1), quarter_of(tokens, 3)])
    far_left = lax.ppermute(left_a, "ctx", [(1, 2), (2, 3)])
    far_right = lax.ppermute(right_a, "ctx", [(2, 1), (1, 0)])
    full_qkv, got_qkv = fsdp_whole(w_qkv, 1)
    own_out, got_out = fsdp_whole(tie(w_out, got_qkv), 1)
    full_vectors, _ = fsdp_whole(jnp.concatenate([tie(gains, got_qkv), shifts]), 1)
    full_up, got_up = fsdp_whole(tie(w_up, got_qkv), 0)
    full_down, got_down = fsdp_whole(tie(w_down, got_qkv), 1)
    full_vectors = full_vectors.astype(f32)
    gain = full_vectors[:2]
    shift = full_vectors[2:]

    positions = jnp.stack([t ^ r for r in order]) * quarter
    chunks = jnp.stack([place, place - 1, place + 1, place ^ 2]) * tok_rows
    info = jnp.concatenate(
        [
            jnp.cumsum(lengths[0]),
            place * tok_rows + positions,
            (chunks[:, None] + positions[None, :]).reshape(-1),
        ]
    ).astype(jnp.int32)

    w_q, w_k, w_v = full_qkv[0], full_qkv[1], full_qkv[2]
    w_all = jnp.concatenate([w_q, w_k, w_v], axis=1)
    w_kv = w_all[:, width:]
    own = [nn(rows, w_all).astype(bf16) for rows in (half_a, half_b)]
    left_b, right_b = tp_swap(left_a, 1), tp_swap(right_a, 1)
    near = [nn(rows, w_kv).astype(bf16) for rows in (left_a, left_b, right_a, right_b)]
    queries = jnp.concatenate([part[:, :width] for part in own])
    own_at, other_at = (width, 2 * width), (0, width)
    near_at = (own_at,) * 2 + (other_at,) * 4
    state = attend(info, queries, own + near, near_at, 7)
    out_y = tp_swap(own_out, 2)
    out_rows = (own_out, out_y, tp_swap(own_out, 1), tp_swap(out_y, 1))
    far_left, far_right = gate((far_left, far_right), state[0], got_up, got_down, *out_rows)
    far_a = jnp.where(place >= 2, far_left, far_right)
    far_b = tp_swap(far_a, 1)
    far = [nn(rows, w_kv).astype(bf16) for rows in (far_a, far_b)]
    context, log_totals = attend(info, queries, far, (other_at,) * 2, 19, state, True)

    pieces = jnp.split(context, 4)
    arrived = [pieces[0]] + [tp_swap(pieces[n], order[n]) for n in (1, 2, 3)]
    resid_rows = quarter_of(tokens, 0).astype(f32)
    for piece, rows in zip(arrived, out_rows):
        resid_rows = resid_rows + nn(piece, rows)
    normed_first, inverse_first = norm_rows(resid_rows)
    hidden = normed_first * gain[0] + shift[0]
    hid0 = hidden.astype(bf16)
    hid2, hid1 = tp_swap(hid0, 2), tp_swap(hid0, 1)
    hid_near = jnp.concatenate([hid0, hid1])
    act_near, slope_near = gelu_pair(nn(hid_near, full_up))
    terms_near = nn(act_near, full_down)
    hid2, terms_near = gate((hid2, terms_near))
    hid_far = jnp.concatenate([hid2, tp_swap(hid2, 1)])
    act_far, slope_far = gelu_pair(nn(hid_far, full_up))
    terms_far = nn(act_far, full_down)
    ffn_rows = rows_in(
        (terms_near[:quarter], terms_near[quarter:], terms_far[:quarter], terms_far[quarter:])
    )
    normed_second, inverse_second = norm_rows(hidden + ffn_rows)
    result = (normed_second * gain[1] + shift[1]).astype(bf16)
    grad_rows = quarter_of(out_grad, 0).astype(f32)
    grad_mid = norm_back(grad_rows, gain[1], normed_second, inverse_second)

    mid0 = grad_mid.astype(bf16)
    mid2, mid1 = tp_swap(mid0, 2), tp_swap(mid0, 1)
    mid_near = jnp.concatenate([mid0, mid1])
    pre_near = (nt(mid_near, full_down) * slope_near).astype(bf16)
    terms_near = nt(pre_near, full_up)
    mid2, terms_near = gate((mid2, terms_near))
    mid_far = jnp.concatenate([mid2, tp_swap(mid2, 1)])

    def column_block(*pairs):
        return lambda start, size: sum(
            tn(left, lax.dynamic_slice_in_dim(right, start, size, axis=1)) for left, right in pairs
        )

    def row_block(*pairs):
        return lambda start, size: sum(
            tn(lax.dynamic_slice_in_dim(left, start, size, axis=1), right) for left, right in pairs
        )

    down_terms, down_send = fsdp_send(
        column_block((act_near, mid_near), (act_far, mid_far)), depth, 1
    )
    down_got = fsdp_swap(down_send)

    pre_far = (nt(mid_far, full_down) * slope_far).astype(bf16)
    terms_far = nt(pre_far, full_up)
    hidden_grad = grad_mid + rows_in(
        (terms_near[:quarter], terms_near[quarter:], terms_far[:quarter], terms_far[quarter:])
    )
    up_terms, up_send = fsdp_send(row_block((hid_near, pre_near), (hid_far, pre_far)), depth, 0)
    resid_grad = norm_back(hidden_grad, gain[0], normed_first, inverse_first)
    attn_own = resid_grad.astype(bf16)

    attn_own, up_send, down_got = gate((attn_own, up_send, down_got))
    up_got = fsdp_swap(up_send)
    down_terms = down_terms + down_got.astype(f32)
    share = up_terms.shape[0]
    down_terms = jnp.concatenate(jnp.split(down_terms, depth // share), axis=1)
    down_kept, send = ctx_split(down_terms, 1)
    down_got = ctx_swap(send, 1)
    pieces = [nt(attn_own, rows).astype(bf16) for rows in out_rows]
    context_grad = jnp.concatenate(
        [pieces[0]] + [tp_swap(pieces[n], order[n]) for n in (1, 2, 3)]
    )

    vectors = jnp.stack(
        [
            jnp.sum(hidden_grad * normed_first, axis=0),
            jnp.sum(grad_rows * normed_second, axis=0),
            jnp.sum(hidden_grad, axis=0),
            jnp.sum(grad_rows, axis=0),
        ]
    )
    spread = jnp.concatenate(
        [attn_own, result, jnp.pad(vectors, ((0, PAD_ROWS - 4), (0, 0))).astype(bf16)]
    )
    context_grad, spread, down_got = gate((context_grad, spread, down_got))
    down_kept, send = ctx_split(down_kept + down_got.astype(f32), 2)
    down_got = ctx_swap(send, 2)
    spread_far, spread_near = tp_swap(spread, 2), tp_swap(spread, 1)

    sources = own + near + far
    sources_at = (own_at,) * 2 + (other_at,) * 6
    part = width // 2
    dq_1, own_1, left_1, right_1, far_1 = attend_back(
        info, queries, context_grad, context, log_totals, sources, sources_at, 7, 0, part
    )
    info_2, far_1, left_1, right_1, down_got, up_got, spread_far = gate(
        (info, far_1, left_1, right_1, down_got, up_got, spread_far), spread_near
    )
    spread_both = tp_swap(spread_far, 1)

    def home(left_kv, right_kv, far_kv):
        return (
            ctx_swap(far_kv, 2),
            lax.ppermute(left_kv, "ctx", [(3, 2), (2, 1), (1, 0)]),
            lax.ppermute(right_kv, "ctx", [(0, 1), (1, 2), (2, 3)]),
        )

    home_1 = home(left_1, right_1, far_1)
    up_kept, up_send = ctx_split(up_terms + up_got.astype(f32), 1)
    down_total = lax.optimization_barrier((down_kept + down_got.astype(f32)).astype(bf16))
    info_2, up_send, down_total = gate((info_2, up_send, down_total), spread_both)
    up_got = ctx_swap(up_send, 1)
    down_got = ctx_swap(down_total, 2)

    dq_2, own_2, left_2, right_2, far_2 = attend_back(
        info_2, queries, context_grad, context, log_totals, sources, sources_at, 7, 1, part
    )
    (
        far_2, left_2, right_2, down_got, up_got, *home_1,
        own_1, own_2, dq_1, dq_2, left_1, right_1, far_1,
        spread, spread_near, spread_far, spread_both,
    ) = gate(
        (
            far_2, left_2, right_2, down_got, up_got, *home_1,
            own_1, own_2, dq_1, dq_2, left_1, right_1, far_1,
            spread, spread_near, spread_far, spread_both,
        )
    )
    home_2 = home(left_2, right_2, far_2)
    up_kept, send = ctx_split(up_kept + up_got.astype(f32), 2)
    up_got = ctx_swap(send, 2)

    held = (spread, spread_near, spread_far, spread_both)
    result_parts = [x[quarter : 2 * quarter] for x in held]
    attn_all = jnp.concatenate([held[n][:quarter] for n in order])
    vectors = sum(x[2 * quarter :].astype(f32) for x in held)

    def rest_of(qkv_terms, start, size):
        right = lax.dynamic_slice_in_dim(attn_all, start, size, axis=1)
        extra = lax.dynamic_slice_in_dim(vectors, start, size, axis=1)
        rows = qkv_terms.shape[0]
        terms = tn(context, right).astype(qkv_terms.dtype).reshape(rows, -1)
        terms = jnp.concatenate([qkv_terms, terms], axis=1)
        extra = jnp.pad(extra, ((0, PAD_ROWS), (0, terms.shape[1] - size)))
        return jnp.concatenate([terms, extra.astype(terms.dtype)])

    pairs = (own_1, own_2, left_1, left_2, right_1, right_2, far_1, far_2)
    rows = (half_a, half_b, left_a, left_b, right_a, right_b, far_a, far_b)
    if lax.axis_size("fsdp") == 2:
        mine = lax.axis_index("fsdp")
        picks = jnp.stack([1 - mine, mine]).astype(jnp.int32)
        half = depth // 2
        qkv_send, qkv_terms = qkv_terms_of(rows, (dq_1, dq_2), pairs, picks, bf16)
        rest_got = fsdp_swap(rest_of(qkv_send, (1 - mine) * half, half))
        rest = rest_of(qkv_terms, mine * half, half)
    else:
        halves = qkv_terms_of(rows, (dq_1, dq_2), pairs, jnp.arange(2, dtype=jnp.int32), f32)
        qkv_terms = lax.psum_scatter(
            jnp.concatenate(halves), "fsdp", scatter_dimension=0, tiled=True
        )
        out_terms = lax.psum_scatter(
            jnp.concatenate([tn(context, attn_all), vectors]), "fsdp",
            scatter_dimension=1, tiled=True,
        )
        rest = jnp.concatenate(
            [qkv_terms, out_terms[:width].reshape(qkv_terms.shape[0], -1)], axis=1
        )
        extra = out_terms[width:]
        extra = jnp.pad(extra, ((0, PAD_ROWS), (0, rest.shape[1] - extra.shape[1])))
        rest = jnp.concatenate([rest, extra])
        rest_got = jnp.zeros(rest.shape, bf16)
    query_grad = jnp.concatenate([dq_1, dq_2], axis=1)

    def owned(own_kv, arrivals):
        total = own_kv.astype(f32)
        for arrival in arrivals:
            total = total + arrival.astype(f32)
        return total.astype(bf16)

    total_1 = owned(own_1, home_1)
    input_terms = (
        nt(query_grad, w_q) + nt(total_1[0], w_k[:, :part]) + nt(total_1[1], w_v[:, :part])
    )
    *home_2, rest_got, up_got = gate((*home_2, rest_got, up_got), input_terms)
    total_2 = owned(own_2, home_2)
    terms = input_terms + nt(total_2[0], w_k[:, part:]) + nt(total_2[1], w_v[:, part:])
    q0, q2, q1, q3 = jnp.split(terms, 4)
    toward = q2 + tp_swap(q3.astype(bf16), 1).astype(f32)
    input_got = tp_swap(toward.astype(bf16), 2)
    here = q0 + tp_swap(q1.astype(bf16), 1).astype(f32)
    up_total = lax.optimization_barrier((up_kept + up_got.astype(f32)).astype(bf16))
    up_got = ctx_swap(up_total, 2)
    out_shape = (width, depth // lax.axis_size("fsdp"))
    rest = rest + rest_got.astype(f32)
    fourth = rest.shape[0] // 4

    def fourth_of(shift):
        return lax.dynamic_slice_in_dim(rest, (place ^ shift) * fourth, fourth)

    rest_kept = fourth_of(0)
    rest_got = [ctx_swap(fourth_of(shift).astype(bf16), shift) for shift in (1, 2, 3)]

    input_got, up_got, *rest_got = gate((input_got, up_got, *rest_got))
    input_own = (resid_grad + here + input_got.astype(f32)).astype(bf16)
    input_far, input_near = tp_swap(input_own, 2), tp_swap(input_own, 1)
    for got in rest_got:
        rest_kept = rest_kept + got.astype(f32)
    rest_total = lax.optimization_barrier(rest_kept.astype(bf16))
    rest_parts = (rest_total, *(ctx_swap(rest_total, shift) for shift in (1, 2, 3)))
    ffn_total = jnp.concatenate(
        [ctx_join(down_total, down_got, 2), ctx_join(up_total, up_got, 2)]
    )
    ffn_got = ctx_swap(ffn_total, 1)
    input_parts = (input_own, input_near, input_far, tp_swap(input_far, 1))
    down_grad, up_grad = (
        ctx_join(total, got, 1).astype(f32)
        for total, got in zip(jnp.split(ffn_total, 2), jnp.split(ffn_got, 2))
    )
    down_grad = jnp.concatenate(jnp.split(down_grad, depth // down_grad.shape[0], axis=1))
    rest_total = natural(rest_parts, (place & 1) == 1, (place >> 1) == 1).astype(f32)
    qkv_grad = jnp.stack([rest_total[:share, n * width : (n + 1) * width] for n in range(3)])
    out_proj_grad = rest_total[:share, 3 * width :].reshape(out_shape)
    vectors = rest_total[share : share + 4, : out_shape[1]]
    return (
        natural(result_parts, core, y),
        natural(input_parts, core, y),
        qkv_grad,
        out_proj_grad,
        up_grad,
        down_grad,
        vectors[:2],
        vectors[2:],
    )


def solution(mesh):
    return jax.shard_map(
        body,
        mesh=mesh,
        in_specs=(
            P(("fsdp", "ctx"), None),
            P(None, "fsdp", "tp"),
            P("tp", "fsdp"),
            P("fsdp", "tp"),
            P("tp", "fsdp"),
            P(None, "fsdp"),
            P(None, "fsdp"),
            P("fsdp", None),
            P(("fsdp", "ctx"), None),
        ),
        out_specs=(
            P(("fsdp", "ctx"), None),
            P(("fsdp", "ctx"), None),
            P(None, "fsdp", "tp"),
            P("tp", "fsdp"),
            P("fsdp", "tp"),
            P("tp", "fsdp"),
            P(None, "fsdp"),
            P(None, "fsdp"),
        ),
        check_vma=False,
    )
```

```python
import functools
import math

import jax
import jax.numpy as jnp
from jax import lax
from jax.experimental import pallas as pl
from jax.experimental.pallas import tpu as pltpu
from jax.sharding import PartitionSpec as P

HEAD_DIM = 64
BLK = 256
PAD_ROWS = 16
LOW = -1e30
norm_eps = 1e-12
f32 = jnp.float32
bf16 = jnp.bfloat16


def contract(left, right, left_dim, right_dim):
    return lax.dot_general(
        left, right, (((left_dim,), (right_dim,)), ((), ())), preferred_element_type=f32
    )


def nn(left, right):
    return contract(left, right, 1, 0)


def nt(left, right):
    return contract(left, right, 1, 1)


def tn(left, right):
    return contract(left, right, 0, 0)


def row_limits(info, qbase, rows):
    end0, end1, end2 = info[0], info[1], info[2]
    pos = qbase + lax.broadcasted_iota(jnp.int32, (1, rows), 1)
    first = jnp.where(pos < end0, 0, jnp.where(pos < end1, end0, end1))
    last = jnp.where(pos < end0, end0, jnp.where(pos < end1, end1, end2))
    real = pos < end2
    return jnp.where(real, first, 0), jnp.where(real, last, 0), real


def key_range(info, qbase, rows):
    end0, end1, end2 = info[0], info[1], info[2]
    low = jnp.where(
        qbase < end0,
        0,
        jnp.where(qbase < end1, end0, jnp.where(qbase < end2, end1, 1 << 30)),
    )
    final = qbase + rows - 1
    high = jnp.where(final < end0, end0, jnp.where(final < end1, end1, end2))
    return low, high


def stage(sources, offsets, width, k_sc, v_sc, sems):
    copies = []
    start = 0
    for n, (source, (k_at, v_at)) in enumerate(zip(sources, offsets)):
        size = source.shape[0]
        for m, (at, target) in enumerate(((k_at, k_sc), (v_at, v_sc))):
            copies.append(
                pltpu.make_async_copy(
                    source.at[:, pl.ds(at, width)],
                    target.at[pl.ds(start, size), :],
                    sems.at[2 * n + m],
                )
            )
        start += size
    for copy in copies:
        copy.start()
    for copy in copies:
        copy.wait()


def transposed(source, target, count):
    def step(j, carry):
        span = pl.ds(pl.multiple_of(j * BLK, BLK), BLK)
        target[:, span] = source[span, :].T
        return carry

    lax.fori_loop(0, count, step, 0)


def masked_heads(block, target, heads):
    rows = block.shape[0]
    head_of = lax.broadcasted_iota(jnp.int32, block.shape, 1) // HEAD_DIM
    for h in range(heads):
        target[h * rows : (h + 1) * rows, :] = jnp.where(head_of == h, block, jnp.zeros_like(block))


def attend_kernel(heads, kcount, kfirst, opens, closes, offsets, info, q_ref, *refs):
    count = len(offsets)
    sources, refs = refs[:count], refs[count:]
    if not opens:
        (m_in, l_in, acc_in), refs = refs[:3], refs[3:]
    if closes:
        (ctx_ref, lse_ref), refs = refs[:2], refs[2:]
    else:
        (m_out, l_out, acc_out), refs = refs[:3], refs[3:]
    m_sc, l_sc, acc_sc, qm_sc, k_sc, v_sc, vt_sc, sems = refs
    i = pl.program_id(0)
    rows, width = q_ref.shape
    qbase = info[3 + i]
    first, last, real = row_limits(info, qbase, rows)
    low, high = key_range(info, qbase, rows)
    factor = math.log2(math.e) / math.sqrt(HEAD_DIM)

    @pl.when(i == 0)
    def _():
        stage(sources, offsets, width, k_sc, v_sc, sems)
        transposed(v_sc, vt_sc, kcount)

    if opens:
        m_sc[...] = jnp.full_like(m_sc, LOW)
        l_sc[...] = jnp.zeros_like(l_sc)
        acc_sc[...] = jnp.zeros_like(acc_sc)
    else:
        m_sc[...] = m_in[...]
        l_sc[...] = l_in[...]
        acc_sc[...] = acc_in[...]
    masked_heads(q_ref[...], qm_sc, heads)
    span_of = [slice(h * HEAD_DIM, (h + 1) * HEAD_DIM) for h in range(heads)]

    def step(j, carry):
        base = info[kfirst + j]

        @pl.when((base + BLK > low) & (base < high))
        def _():
            span = pl.ds(pl.multiple_of(j * BLK, BLK), BLK)
            kb = k_sc[span, :]
            vt = vt_sc[:, span]
            posk = base + lax.broadcasted_iota(jnp.int32, (BLK, rows), 0)
            allowed = (posk >= first) & (posk < last)
            s = [
                jnp.where(allowed, nt(kb, qm_sc[h * rows : (h + 1) * rows, :]) * factor, LOW)
                for h in range(heads)
            ]
            m_old = m_sc[...]
            m_new = [
                jnp.maximum(m_old[h : h + 1, :], jnp.max(s[h], axis=0, keepdims=True))
                for h in range(heads)
            ]
            alpha = [jnp.exp2(m_old[h : h + 1, :] - m_new[h]) for h in range(heads)]
            p = [jnp.exp2(s[h] - m_new[h]) for h in range(heads)]
            sums = [jnp.sum(p[h], axis=0, keepdims=True) for h in range(heads)]
            pv = [nn(vt[span_of[h], :], p[h].astype(bf16)) for h in range(heads)]
            m_sc[...] = jnp.concatenate(m_new)
            l_sc[...] = l_sc[...] * jnp.concatenate(alpha) + jnp.concatenate(sums)
            for h in range(heads):
                acc_sc[span_of[h], :] = acc_sc[span_of[h], :] * alpha[h] + pv[h]

        return carry

    lax.fori_loop(0, kcount, step, 0)
    if closes:
        for h in range(heads):
            total = l_sc[h : h + 1, :]
            acc_sc[span_of[h], :] = jnp.where(real, acc_sc[span_of[h], :] / total, 0.0)
            lse_ref[h : h + 1, :] = jnp.where(real, m_sc[h : h + 1, :] + jnp.log2(total), -LOW)
        ctx_ref[...] = acc_sc[...].T.astype(bf16)
    else:
        m_out[...] = m_sc[...]
        l_out[...] = l_sc[...]
        acc_out[...] = acc_sc[...]


def whole(shape):
    return pl.BlockSpec(shape, lambda i, *_: (0,) * len(shape))


def attend(info, q, sources, offsets, kfirst, state=None, closes=False):
    rows, width = q.shape
    heads = width // HEAD_DIM
    keys = sum(source.shape[0] for source in sources)
    opens = state is None
    block = pl.BlockSpec((BLK, width), lambda i, *_: (i, 0))
    per_head = pl.BlockSpec((heads, BLK), lambda i, *_: (0, i))
    per_feature = pl.BlockSpec((width, BLK), lambda i, *_: (0, i))
    stats = jax.ShapeDtypeStruct((heads, rows), f32)
    carried = [per_head, per_head, per_feature]
    return pl.pallas_call(
        functools.partial(attend_kernel, heads, keys // BLK, kfirst, opens, closes, offsets),
        grid_spec=pltpu.PrefetchScalarGridSpec(
            num_scalar_prefetch=1,
            grid=(rows // BLK,),
            in_specs=[block]
            + [pl.BlockSpec(memory_space=pl.ANY)] * len(sources)
            + ([] if opens else carried),
            out_specs=[block, per_head] if closes else carried,
            scratch_shapes=[
                pltpu.VMEM((heads, BLK), f32),
                pltpu.VMEM((heads, BLK), f32),
                pltpu.VMEM((width, BLK), f32),
                pltpu.VMEM((heads * BLK, width), bf16),
                pltpu.VMEM((keys, width), bf16),
                pltpu.VMEM((keys, width), bf16),
                pltpu.VMEM((width, keys), bf16),
                pltpu.SemaphoreType.DMA((2 * len(sources),)),
            ],
        ),
        out_shape=[jax.ShapeDtypeStruct((rows, width), bf16), stats]
        if closes
        else [stats, stats, jax.ShapeDtypeStruct((width, rows), f32)],
        cost_estimate=pl.CostEstimate(flops=1024, bytes_accessed=1024, transcendentals=0),
        name="attend_near" if opens else "attend_far",
    )(info, q, *sources, *(() if opens else state))


def attend_back_kernel(
    heads, kcount, kfirst, offsets, info, q_ref, do_ref, o_ref, lse_ref, *refs
):
    count = len(offsets)
    sources, refs = refs[:count], refs[count:]
    dq_ref, *outs = refs[:5]
    dk_sc, dv_sc, dqt_sc, qm_sc, dom_sc, delta_sc, k_sc, v_sc, kt_sc, sems = refs[5:]
    i = pl.program_id(0)
    rows, width = q_ref.shape
    qbase = info[3 + i]
    first, last, real = row_limits(info, qbase, rows)
    low, high = key_range(info, qbase, rows)
    scale = 1.0 / math.sqrt(HEAD_DIM)
    factor = math.log2(math.e) * scale

    @pl.when(i == 0)
    def _():
        dk_sc[...] = jnp.zeros_like(dk_sc)
        dv_sc[...] = jnp.zeros_like(dv_sc)
        stage(sources, offsets, width, k_sc, v_sc, sems)
        transposed(k_sc, kt_sc, kcount)

    dqt_sc[...] = jnp.zeros_like(dqt_sc)
    do = do_ref[...]
    masked_heads(q_ref[...], qm_sc, heads)
    masked_heads(do, dom_sc, heads)
    prod = (do.astype(f32) * o_ref[...].astype(f32)).T
    span_of = [slice(h * HEAD_DIM, (h + 1) * HEAD_DIM) for h in range(heads)]
    rows_of = [slice(h * rows, (h + 1) * rows) for h in range(heads)]
    for h in range(heads):
        delta_sc[h : h + 1, :] = jnp.sum(prod[span_of[h], :], axis=0, keepdims=True)

    def step(j, carry):
        base = info[kfirst + j]

        @pl.when((base + BLK > low) & (base < high))
        def _():
            span = pl.ds(pl.multiple_of(j * BLK, BLK), BLK)
            kb = k_sc[span, :]
            vb = v_sc[span, :]
            kt = kt_sc[:, span]
            posk = base + lax.broadcasted_iota(jnp.int32, (BLK, rows), 0)
            allowed = (posk >= first) & (posk < last)
            s = [nt(kb, qm_sc[rows_of[h], :]) for h in range(heads)]
            dp = [nt(vb, dom_sc[rows_of[h], :]) for h in range(heads)]
            p = [
                jnp.where(allowed, jnp.exp2(s[h] * factor - lse_ref[0, h : h + 1, :]), 0.0)
                for h in range(heads)
            ]
            ds = [(p[h] * (dp[h] - delta_sc[h : h + 1, :])).astype(bf16) for h in range(heads)]
            low_p = [p[h].astype(bf16) for h in range(heads)]
            dv_sc[span, :] += nn(jnp.concatenate(low_p, axis=1), dom_sc[...])
            dk_sc[span, :] += nn(jnp.concatenate(ds, axis=1), qm_sc[...])
            for h in range(heads):
                dqt_sc[span_of[h], :] += nn(kt[span_of[h], :], ds[h])

        return carry

    lax.fori_loop(0, kcount, step, 0)
    dq_ref[...] = (dqt_sc[...] * scale).T.astype(bf16)

    @pl.when(i == pl.num_programs(0) - 1)
    def _():
        part = outs[0].shape[1]
        for n, out_ref in enumerate(outs):
            out_ref[0] = (dk_sc[n * part : (n + 1) * part, :] * scale).astype(bf16)
            out_ref[1] = dv_sc[n * part : (n + 1) * part, :].astype(bf16)


def attend_back(info, q, do, o, lse, sources, offsets, kfirst, pick, width):
    rows = q.shape[0]
    heads = width // HEAD_DIM
    keys = sum(source.shape[0] for source in sources)
    block = pl.BlockSpec((BLK, width), lambda i, *_: (i, pick))
    pair = (2, keys // 4, width)
    offsets = tuple((k_at + pick * width, v_at + pick * width) for k_at, v_at in offsets)
    return pl.pallas_call(
        functools.partial(attend_back_kernel, heads, keys // BLK, kfirst, offsets),
        grid_spec=pltpu.PrefetchScalarGridSpec(
            num_scalar_prefetch=1,
            grid=(rows // BLK,),
            in_specs=[
                block,
                block,
                block,
                pl.BlockSpec((1, heads, BLK), lambda i, *_: (pick, 0, i)),
            ]
            + [pl.BlockSpec(memory_space=pl.ANY)] * len(sources),
            out_specs=[pl.BlockSpec((BLK, width), lambda i, *_: (i, 0))] + [whole(pair)] * 4,
            scratch_shapes=[
                pltpu.VMEM((keys, width), f32),
                pltpu.VMEM((keys, width), f32),
                pltpu.VMEM((width, BLK), f32),
                pltpu.VMEM((heads * BLK, width), bf16),
                pltpu.VMEM((heads * BLK, width), bf16),
                pltpu.VMEM((heads, BLK), f32),
                pltpu.VMEM((keys, width), bf16),
                pltpu.VMEM((keys, width), bf16),
                pltpu.VMEM((width, keys), bf16),
                pltpu.SemaphoreType.DMA((2 * len(sources),)),
            ],
        ),
        out_shape=[jax.ShapeDtypeStruct((rows, width), bf16)]
        + [jax.ShapeDtypeStruct(pair, bf16)] * 4,
        cost_estimate=pl.CostEstimate(flops=1024, bytes_accessed=1024, transcendentals=0),
        name="attend_back",
    )(info, q, do, o, lse.reshape(-1, heads, rows), *sources)


def qkv_terms_kernel(order, *refs):
    rows, (dq_1, dq_2), pairs = refs[:8], refs[8:10], refs[10:18]
    sent_ref, mine_ref = refs[18:]
    size = rows[0].shape[0]
    query, key_value = None, None
    for n, rows_ref in enumerate(rows):
        left = rows_ref[...]
        span = slice((n % 2) * size, (n % 2 + 1) * size)
        first, second = pairs[n // 2 * 2], pairs[n // 2 * 2 + 1]
        grads = jnp.concatenate(
            [first[0, span], second[0, span], first[1, span], second[1, span]], axis=1
        )
        term = tn(left, grads)
        key_value = term if key_value is None else key_value + term
        if n < 2:
            term = tn(left, jnp.concatenate([dq_1[span], dq_2[span]], axis=1))
            query = term if query is None else query + term
    total = jnp.concatenate([query, key_value], axis=1)

    @pl.when(pl.program_id(0) == 0)
    def _():
        sent_ref[...] = total.astype(sent_ref.dtype)

    @pl.when(pl.program_id(0) == 1)
    def _():
        mine_ref[...] = total


def qkv_terms_of(rows, queries, pairs, order, sent_type):
    size, depth = rows[0].shape
    half = depth // 2
    wide = 2 * (queries[0].shape[1] + 2 * pairs[0].shape[2])
    return pl.pallas_call(
        qkv_terms_kernel,
        grid_spec=pltpu.PrefetchScalarGridSpec(
            num_scalar_prefetch=1,
            grid=(2,),
            in_specs=[pl.BlockSpec((size, half), lambda i, pick: (0, pick[i]))] * 8
            + [whole(x.shape) for x in (*queries, *pairs)],
            out_specs=[whole((half, wide)), whole((half, wide))],
        ),
        out_shape=[
            jax.ShapeDtypeStruct((half, wide), sent_type),
            jax.ShapeDtypeStruct((half, wide), f32),
        ],
        cost_estimate=pl.CostEstimate(flops=1024, bytes_accessed=1024, transcendentals=0),
        name="qkv_terms",
    )(order, *rows, *queries, *pairs)


def tp_swap(x, bit):
    return lax.ppermute(x, "tp", [(i, i ^ bit) for i in range(4)])


def gate_kernel(*refs):
    pass


def gate(through, *waits):
    through = tuple(through)
    anywhere = pl.BlockSpec(memory_space=pl.ANY)
    return pl.pallas_call(
        gate_kernel,
        in_specs=[anywhere] * (len(through) + len(waits)),
        out_specs=[anywhere] * len(through),
        out_shape=[jax.ShapeDtypeStruct(x.shape, x.dtype) for x in through],
        input_output_aliases={n: n for n in range(len(through))},
        name="gate",
    )(*through, *waits)


def tie(x, *others):
    for other in others:
        x = x + (other[(0,) * other.ndim].astype(f32) * 0.0).astype(x.dtype)
    return x


def fsdp_whole(shard, dim):
    if lax.axis_size("fsdp") != 2:
        full = lax.all_gather(shard, "fsdp", axis=dim, tiled=True)
        return full, full
    other = lax.ppermute(shard, "fsdp", [(0, 1), (1, 0)])
    low_half = lax.axis_index("fsdp") == 0
    return jnp.concatenate(
        [jnp.where(low_half, shard, other), jnp.where(low_half, other, shard)], axis=dim
    ), other


def fsdp_send(block_of, size, dim):
    if lax.axis_size("fsdp") != 2:
        mine = lax.psum_scatter(block_of(0, size), "fsdp", scatter_dimension=dim, tiled=True)
        return mine, jnp.zeros(mine.shape, bf16)
    half = size // 2
    place = lax.axis_index("fsdp")
    return block_of(place * half, half), block_of((1 - place) * half, half).astype(bf16)


def fsdp_swap(x):
    if lax.axis_size("fsdp") != 2:
        return x
    return lax.ppermute(x, "fsdp", [(0, 1), (1, 0)])


def ctx_swap(x, bit):
    return lax.ppermute(x, "ctx", [(i, i ^ bit) for i in range(4)])


def ctx_split(terms, bit):
    upper = (lax.axis_index("ctx") & bit) != 0
    size = terms.shape[0] // 2
    low_half, high_half = terms[:size], terms[size:]
    return (
        jnp.where(upper, high_half, low_half),
        jnp.where(upper, low_half, high_half).astype(bf16),
    )


def ctx_join(total, got, bit):
    upper = (lax.axis_index("ctx") & bit) != 0
    return jnp.concatenate([jnp.where(upper, got, total), jnp.where(upper, total, got)])


def rows_out(own):
    far = tp_swap(own, 2)
    near = tp_swap(own, 1)
    return own, near, far, tp_swap(far, 1)


def rows_in(terms):
    toward = terms[2] + tp_swap(terms[3].astype(bf16), 1).astype(f32)
    got = tp_swap(toward.astype(bf16), 2)
    here = terms[0] + tp_swap(terms[1].astype(bf16), 1).astype(f32)
    return here + got.astype(f32)


def natural(parts, core, y):
    r0, r1, r2, r3 = parts
    a0, a1 = jnp.where(core, r1, r0), jnp.where(core, r0, r1)
    a2, a3 = jnp.where(core, r3, r2), jnp.where(core, r2, r3)
    return jnp.concatenate(
        [jnp.where(y, a2, a0), jnp.where(y, a3, a1), jnp.where(y, a0, a2), jnp.where(y, a1, a3)]
    )


def norm_rows(rows):
    centre = rows - jnp.mean(rows, axis=-1, keepdims=True)
    inverse = lax.rsqrt(jnp.mean(centre * centre, axis=-1, keepdims=True) + norm_eps)
    return centre * inverse, inverse


def norm_back(grad, gain, normed, inverse):
    dn = grad * gain
    return (
        dn
        - jnp.mean(dn, axis=-1, keepdims=True)
        - normed * jnp.mean(dn * normed, axis=-1, keepdims=True)
    ) * inverse


def gelu_pair(values):
    phi_sum = 0.5 + 0.5 * lax.erf(values * math.sqrt(0.5))
    density = jnp.exp(values * values * -0.5) * (1.0 / math.sqrt(2.0 * math.pi))
    return (values * phi_sum).astype(bf16), phi_sum + values * density


def body(tokens, w_qkv, w_out, w_up, w_down, gains, shifts, lengths, out_grad):
    place = lax.axis_index("ctx")
    t = lax.axis_index("tp")
    core, y = (t & 1) == 1, (t >> 1) == 1
    tok_rows, depth = tokens.shape
    width = w_qkv.shape[2]
    quarter = tok_rows // 4
    order = (0, 2, 1, 3)

    def quarter_of(array, r):
        return lax.dynamic_slice_in_dim(array, (t ^ r) * quarter, quarter)

    half_a = jnp.concatenate([quarter_of(tokens, 0), quarter_of(tokens, 2)])
    left_a = lax.ppermute(half_a, "ctx", [(0, 1), (1, 2), (2, 3)])
    right_a = lax.ppermute(half_a, "ctx", [(3, 2), (2, 1), (1, 0)])
    half_b = jnp.concatenate([quarter_of(tokens, 1), quarter_of(tokens, 3)])
    far_left = lax.ppermute(left_a, "ctx", [(1, 2), (2, 3)])
    far_right = lax.ppermute(right_a, "ctx", [(2, 1), (1, 0)])
    full_qkv, got_qkv = fsdp_whole(w_qkv, 1)
    own_out, got_out = fsdp_whole(tie(w_out, got_qkv), 1)
    full_vectors, _ = fsdp_whole(jnp.concatenate([tie(gains, got_qkv), shifts]), 1)
    full_up, got_up = fsdp_whole(tie(w_up, got_qkv), 0)
    full_down, got_down = fsdp_whole(tie(w_down, got_qkv), 1)
    full_vectors = full_vectors.astype(f32)
    gain = full_vectors[:2]
    shift = full_vectors[2:]

    positions = jnp.stack([t ^ r for r in order]) * quarter
    chunks = jnp.stack([place, place - 1, place + 1, place ^ 2]) * tok_rows
    info = jnp.concatenate(
        [
            jnp.cumsum(lengths[0]),
            place * tok_rows + positions,
            (chunks[:, None] + positions[None, :]).reshape(-1),
        ]
    ).astype(jnp.int32)

    w_q, w_k, w_v = full_qkv[0], full_qkv[1], full_qkv[2]
    w_all = jnp.concatenate([w_q, w_k, w_v], axis=1)
    w_kv = w_all[:, width:]
    own = [nn(rows, w_all).astype(bf16) for rows in (half_a, half_b)]
    left_b, right_b = tp_swap(left_a, 1), tp_swap(right_a, 1)
    near = [nn(rows, w_kv).astype(bf16) for rows in (left_a, left_b, right_a, right_b)]
    queries = jnp.concatenate([part[:, :width] for part in own])
    own_at, other_at = (width, 2 * width), (0, width)
    near_at = (own_at,) * 2 + (other_at,) * 4
    state = attend(info, queries, own + near, near_at, 7)
    out_y = tp_swap(own_out, 2)
    out_rows = (own_out, out_y, tp_swap(own_out, 1), tp_swap(out_y, 1))
    far_left, far_right = gate((far_left, far_right), state[0], got_up, got_down, *out_rows)
    far_a = jnp.where(place >= 2, far_left, far_right)
    far_b = tp_swap(far_a, 1)
    far = [nn(rows, w_kv).astype(bf16) for rows in (far_a, far_b)]
    context, log_totals = attend(info, queries, far, (other_at,) * 2, 19, state, True)

    pieces = jnp.split(context, 4)
    arrived = [pieces[0]] + [tp_swap(pieces[n], order[n]) for n in (1, 2, 3)]
    arrived = gate(arrived, full_up, full_down)
    resid_rows = quarter_of(tokens, 0).astype(f32)
    for piece, rows in zip(arrived, out_rows):
        resid_rows = resid_rows + nn(piece, rows)
    normed_first, inverse_first = norm_rows(resid_rows)
    hidden = normed_first * gain[0] + shift[0]
    hid0 = hidden.astype(bf16)
    hid2, hid1 = tp_swap(hid0, 2), tp_swap(hid0, 1)
    hid_near = jnp.concatenate([hid0, hid1])
    act_near, slope_near = gelu_pair(nn(hid_near, full_up))
    terms_near = nn(act_near, full_down)
    hid2, terms_near = gate((hid2, terms_near))
    hid_far = jnp.concatenate([hid2, tp_swap(hid2, 1)])
    act_far, slope_far = gelu_pair(nn(hid_far, full_up))
    terms_far = nn(act_far, full_down)
    ffn_rows = rows_in(
        (terms_near[:quarter], terms_near[quarter:], terms_far[:quarter], terms_far[quarter:])
    )
    normed_second, inverse_second = norm_rows(hidden + ffn_rows)
    result = (normed_second * gain[1] + shift[1]).astype(bf16)
    grad_rows = quarter_of(out_grad, 0).astype(f32)
    grad_mid = norm_back(grad_rows, gain[1], normed_second, inverse_second)

    mid0 = grad_mid.astype(bf16)
    mid2, mid1 = tp_swap(mid0, 2), tp_swap(mid0, 1)
    mid_near = jnp.concatenate([mid0, mid1])
    pre_near = (nt(mid_near, full_down) * slope_near).astype(bf16)
    terms_near = nt(pre_near, full_up)
    mid2, terms_near = gate((mid2, terms_near))
    mid_far = jnp.concatenate([mid2, tp_swap(mid2, 1)])

    def column_block(*pairs):
        return lambda start, size: sum(
            tn(left, lax.dynamic_slice_in_dim(right, start, size, axis=1)) for left, right in pairs
        )

    def row_block(*pairs):
        return lambda start, size: sum(
            tn(lax.dynamic_slice_in_dim(left, start, size, axis=1), right) for left, right in pairs
        )

    down_terms, down_send = fsdp_send(
        column_block((act_near, mid_near), (act_far, mid_far)), depth, 1
    )
    down_got = fsdp_swap(down_send)

    pre_far = (nt(mid_far, full_down) * slope_far).astype(bf16)
    terms_far = nt(pre_far, full_up)
    hidden_grad = grad_mid + rows_in(
        (terms_near[:quarter], terms_near[quarter:], terms_far[:quarter], terms_far[quarter:])
    )
    up_terms, up_send = fsdp_send(row_block((hid_near, pre_near), (hid_far, pre_far)), depth, 0)
    resid_grad = norm_back(hidden_grad, gain[0], normed_first, inverse_first)
    attn_own = resid_grad.astype(bf16)

    up_send, down_got = gate((up_send, down_got), attn_own)
    up_got = fsdp_swap(up_send)
    down_terms = down_terms + down_got.astype(f32)
    share = up_terms.shape[0]
    down_terms = jnp.concatenate(jnp.split(down_terms, depth // share), axis=1)
    down_kept, send = ctx_split(down_terms, 1)
    down_got = ctx_swap(send, 1)
    pieces = [nt(attn_own, rows).astype(bf16) for rows in out_rows]
    context_grad = jnp.concatenate(
        [pieces[0]] + [tp_swap(pieces[n], order[n]) for n in (1, 2, 3)]
    )

    vectors = jnp.stack(
        [
            jnp.sum(hidden_grad * normed_first, axis=0),
            jnp.sum(grad_rows * normed_second, axis=0),
            jnp.sum(hidden_grad, axis=0),
            jnp.sum(grad_rows, axis=0),
        ]
    )
    spread = jnp.concatenate(
        [attn_own, result, jnp.pad(vectors, ((0, PAD_ROWS - 4), (0, 0))).astype(bf16)]
    )
    context_grad, spread = gate((context_grad, spread))
    spread_far, spread_near = tp_swap(spread, 2), tp_swap(spread, 1)

    sources = own + near + far
    sources_at = (own_at,) * 2 + (other_at,) * 6
    part = width // 2
    dq_1, own_1, left_1, right_1, far_1 = attend_back(
        info, queries, context_grad, context, log_totals, sources, sources_at, 7, 0, part
    )
    info_2, far_1, left_1, right_1, down_got, up_got, spread_far = gate(
        (info, far_1, left_1, right_1, down_got, up_got, spread_far), spread_near
    )
    spread_both = tp_swap(spread_far, 1)

    def home(left_kv, right_kv, far_kv):
        return (
            ctx_swap(far_kv, 2),
            lax.ppermute(left_kv, "ctx", [(3, 2), (2, 1), (1, 0)]),
            lax.ppermute(right_kv, "ctx", [(0, 1), (1, 2), (2, 3)]),
        )

    home_1 = home(left_1, right_1, far_1)
    up_kept, up_send = ctx_split(up_terms + up_got.astype(f32), 1)
    down_kept, down_send = ctx_split(down_kept + down_got.astype(f32), 2)
    info_2, up_send, down_send = gate((info_2, up_send, down_send), spread_both)
    up_got = ctx_swap(up_send, 1)
    down_got = ctx_swap(down_send, 2)

    dq_2, own_2, left_2, right_2, far_2 = attend_back(
        info_2, queries, context_grad, context, log_totals, sources, sources_at, 7, 1, part
    )
    (
        far_2, left_2, right_2, down_got, up_got, *home_1,
        own_1, own_2, dq_1, dq_2, left_1, right_1, far_1,
        spread, spread_near, spread_far, spread_both,
    ) = gate(
        (
            far_2, left_2, right_2, down_got, up_got, *home_1,
            own_1, own_2, dq_1, dq_2, left_1, right_1, far_1,
            spread, spread_near, spread_far, spread_both,
        )
    )
    home_2 = home(left_2, right_2, far_2)
    down_total = lax.optimization_barrier((down_kept + down_got.astype(f32)).astype(bf16))
    up_kept, send = ctx_split(up_kept + up_got.astype(f32), 2)
    ffn_got = ctx_swap(jnp.concatenate([down_total, send]), 2)

    def spread_sums(held):
        return (
            jnp.concatenate([held[n][:quarter] for n in order]),
            sum(x[2 * quarter :].astype(f32) for x in held),
        )

    def rest_of(qkv_terms, start, size):
        right = lax.dynamic_slice_in_dim(attn_all, start, size, axis=1)
        extra = lax.dynamic_slice_in_dim(vectors, start, size, axis=1)
        rows = qkv_terms.shape[0]
        terms = tn(context, right).astype(qkv_terms.dtype).reshape(rows, -1)
        terms = jnp.concatenate([qkv_terms, terms], axis=1)
        extra = jnp.pad(extra, ((0, PAD_ROWS), (0, terms.shape[1] - size)))
        return jnp.concatenate([terms, extra.astype(terms.dtype)])

    pairs = (own_1, own_2, left_1, left_2, right_1, right_2, far_1, far_2)
    rows = (half_a, half_b, left_a, left_b, right_a, right_b, far_a, far_b)
    if lax.axis_size("fsdp") == 2:
        mine = lax.axis_index("fsdp")
        picks = jnp.stack([1 - mine, mine]).astype(jnp.int32)
        half = depth // 2
        qkv_send, qkv_terms = qkv_terms_of(rows, (dq_1, dq_2), pairs, picks, bf16)
        spread, spread_near, spread_far, spread_both = gate(
            (spread, spread_near, spread_far, spread_both), qkv_send
        )
        held = (spread, spread_near, spread_far, spread_both)
        attn_all, vectors = spread_sums(held)
        rest_got = fsdp_swap(rest_of(qkv_send, (1 - mine) * half, half))
        rest = rest_of(qkv_terms, mine * half, half)
    else:
        halves = qkv_terms_of(rows, (dq_1, dq_2), pairs, jnp.arange(2, dtype=jnp.int32), f32)
        qkv_terms = lax.psum_scatter(
            jnp.concatenate(halves), "fsdp", scatter_dimension=0, tiled=True
        )
        held = (spread, spread_near, spread_far, spread_both)
        attn_all, vectors = spread_sums(held)
        out_terms = lax.psum_scatter(
            jnp.concatenate([tn(context, attn_all), vectors]), "fsdp",
            scatter_dimension=1, tiled=True,
        )
        rest = jnp.concatenate(
            [qkv_terms, out_terms[:width].reshape(qkv_terms.shape[0], -1)], axis=1
        )
        extra = out_terms[width:]
        extra = jnp.pad(extra, ((0, PAD_ROWS), (0, rest.shape[1] - extra.shape[1])))
        rest = jnp.concatenate([rest, extra])
        rest_got = jnp.zeros(rest.shape, bf16)
    result_parts = [x[quarter : 2 * quarter] for x in held]
    query_grad = jnp.concatenate([dq_1, dq_2], axis=1)

    def owned(own_kv, arrivals):
        total = own_kv.astype(f32)
        for arrival in arrivals:
            total = total + arrival.astype(f32)
        return total.astype(bf16)

    total_1 = owned(own_1, home_1)
    input_terms = (
        nt(query_grad, w_q) + nt(total_1[0], w_k[:, :part]) + nt(total_1[1], w_v[:, :part])
    )
    *home_2, rest_got, ffn_got = gate((*home_2, rest_got, ffn_got), input_terms)
    down_got, up_got = jnp.split(ffn_got, 2)
    total_2 = owned(own_2, home_2)
    terms = input_terms + nt(total_2[0], w_k[:, part:]) + nt(total_2[1], w_v[:, part:])
    q0, q2, q1, q3 = jnp.split(terms, 4)
    toward = q2 + tp_swap(q3.astype(bf16), 1).astype(f32)
    input_got = tp_swap(toward.astype(bf16), 2)
    here = q0 + tp_swap(q1.astype(bf16), 1).astype(f32)
    up_total = lax.optimization_barrier((up_kept + up_got.astype(f32)).astype(bf16))
    up_got = ctx_swap(up_total, 2)
    out_shape = (width, depth // lax.axis_size("fsdp"))
    rest = rest + rest_got.astype(f32)
    fourth = rest.shape[0] // 4

    def fourth_of(shift):
        return lax.dynamic_slice_in_dim(rest, (place ^ shift) * fourth, fourth)

    rest_kept = fourth_of(0)
    rest_got = [ctx_swap(fourth_of(shift).astype(bf16), shift) for shift in (1, 2, 3)]

    input_got, up_got, *rest_got = gate((input_got, up_got, *rest_got))
    input_own = (resid_grad + here + input_got.astype(f32)).astype(bf16)
    input_far, input_near = tp_swap(input_own, 2), tp_swap(input_own, 1)
    for got in rest_got:
        rest_kept = rest_kept + got.astype(f32)
    rest_total = lax.optimization_barrier(rest_kept.astype(bf16))
    rest_parts = (rest_total, *(ctx_swap(rest_total, shift) for shift in (1, 2, 3)))
    ffn_total = jnp.concatenate(
        [ctx_join(down_total, down_got, 2), ctx_join(up_total, up_got, 2)]
    )
    ffn_got = ctx_swap(ffn_total, 1)
    input_parts = (input_own, input_near, input_far, tp_swap(input_far, 1))
    down_grad, up_grad = (
        ctx_join(total, got, 1).astype(f32)
        for total, got in zip(jnp.split(ffn_total, 2), jnp.split(ffn_got, 2))
    )
    down_grad = jnp.concatenate(jnp.split(down_grad, depth // down_grad.shape[0], axis=1))
    rest_total = natural(rest_parts, (place & 1) == 1, (place >> 1) == 1).astype(f32)
    qkv_grad = jnp.stack([rest_total[:share, n * width : (n + 1) * width] for n in range(3)])
    out_proj_grad = rest_total[:share, 3 * width :].reshape(out_shape)
    vectors = rest_total[share : share + 4, : out_shape[1]]
    return (
        natural(result_parts, core, y),
        natural(input_parts, core, y),
        qkv_grad,
        out_proj_grad,
        up_grad,
        down_grad,
        vectors[:2],
        vectors[2:],
    )


def solution(mesh):
    return jax.shard_map(
        body,
        mesh=mesh,
        in_specs=(
            P(("fsdp", "ctx"), None),
            P(None, "fsdp", "tp"),
            P("tp", "fsdp"),
            P("fsdp", "tp"),
            P("tp", "fsdp"),
            P(None, "fsdp"),
            P(None, "fsdp"),
            P("fsdp", None),
            P(("fsdp", "ctx"), None),
        ),
        out_specs=(
            P(("fsdp", "ctx"), None),
            P(("fsdp", "ctx"), None),
            P(None, "fsdp", "tp"),
            P("tp", "fsdp"),
            P("fsdp", "tp"),
            P("tp", "fsdp"),
            P(None, "fsdp"),
            P(None, "fsdp"),
        ),
        check_vma=False,
    )
```

```python
import functools
import math

import jax
import jax.numpy as jnp
from jax import lax
from jax.experimental import pallas as pl
from jax.experimental.pallas import tpu as pltpu
from jax.sharding import PartitionSpec as P

HEAD_DIM = 64
BLK = 256
PAD_ROWS = 16
LOW = -1e30
norm_eps = 1e-12
f32 = jnp.float32
bf16 = jnp.bfloat16


def contract(left, right, left_dim, right_dim):
    return lax.dot_general(
        left, right, (((left_dim,), (right_dim,)), ((), ())), preferred_element_type=f32
    )


def nn(left, right):
    return contract(left, right, 1, 0)


def nt(left, right):
    return contract(left, right, 1, 1)


def tn(left, right):
    return contract(left, right, 0, 0)


def row_limits(info, qbase, rows):
    end0, end1, end2 = info[0], info[1], info[2]
    pos = qbase + lax.broadcasted_iota(jnp.int32, (1, rows), 1)
    first = jnp.where(pos < end0, 0, jnp.where(pos < end1, end0, end1))
    last = jnp.where(pos < end0, end0, jnp.where(pos < end1, end1, end2))
    real = pos < end2
    return jnp.where(real, first, 0), jnp.where(real, last, 0), real


def key_range(info, qbase, rows):
    end0, end1, end2 = info[0], info[1], info[2]
    low = jnp.where(
        qbase < end0,
        0,
        jnp.where(qbase < end1, end0, jnp.where(qbase < end2, end1, 1 << 30)),
    )
    final = qbase + rows - 1
    high = jnp.where(final < end0, end0, jnp.where(final < end1, end1, end2))
    return low, high


def stage(sources, offsets, width, k_sc, v_sc, sems):
    copies = []
    start = 0
    for n, (source, (k_at, v_at)) in enumerate(zip(sources, offsets)):
        size = source.shape[0]
        for m, (at, target) in enumerate(((k_at, k_sc), (v_at, v_sc))):
            copies.append(
                pltpu.make_async_copy(
                    source.at[:, pl.ds(at, width)],
                    target.at[pl.ds(start, size), :],
                    sems.at[2 * n + m],
                )
            )
        start += size
    for copy in copies:
        copy.start()
    for copy in copies:
        copy.wait()


def transposed(source, target, count):
    def step(j, carry):
        span = pl.ds(pl.multiple_of(j * BLK, BLK), BLK)
        target[:, span] = source[span, :].T
        return carry

    lax.fori_loop(0, count, step, 0)


def masked_heads(block, target, heads):
    rows = block.shape[0]
    head_of = lax.broadcasted_iota(jnp.int32, block.shape, 1) // HEAD_DIM
    for h in range(heads):
        target[h * rows : (h + 1) * rows, :] = jnp.where(head_of == h, block, jnp.zeros_like(block))


def attend_kernel(heads, kcount, kfirst, opens, closes, offsets, info, q_ref, *refs):
    count = len(offsets)
    sources, refs = refs[:count], refs[count:]
    if not opens:
        (m_in, l_in, acc_in), refs = refs[:3], refs[3:]
    if closes:
        (ctx_ref, lse_ref), refs = refs[:2], refs[2:]
    else:
        (m_out, l_out, acc_out), refs = refs[:3], refs[3:]
    m_sc, l_sc, acc_sc, qm_sc, k_sc, v_sc, vt_sc, sems = refs
    i = pl.program_id(0)
    rows, width = q_ref.shape
    qbase = info[3 + i]
    first, last, real = row_limits(info, qbase, rows)
    low, high = key_range(info, qbase, rows)
    factor = math.log2(math.e) / math.sqrt(HEAD_DIM)

    @pl.when(i == 0)
    def _():
        stage(sources, offsets, width, k_sc, v_sc, sems)
        transposed(v_sc, vt_sc, kcount)

    if opens:
        m_sc[...] = jnp.full_like(m_sc, LOW)
        l_sc[...] = jnp.zeros_like(l_sc)
        acc_sc[...] = jnp.zeros_like(acc_sc)
    else:
        m_sc[...] = m_in[...]
        l_sc[...] = l_in[...]
        acc_sc[...] = acc_in[...]
    masked_heads(q_ref[...], qm_sc, heads)
    span_of = [slice(h * HEAD_DIM, (h + 1) * HEAD_DIM) for h in range(heads)]

    def step(j, carry):
        base = info[kfirst + j]

        @pl.when((base + BLK > low) & (base < high))
        def _():
            span = pl.ds(pl.multiple_of(j * BLK, BLK), BLK)
            kb = k_sc[span, :]
            vt = vt_sc[:, span]
            posk = base + lax.broadcasted_iota(jnp.int32, (BLK, rows), 0)
            allowed = (posk >= first) & (posk < last)
            s = [
                jnp.where(allowed, nt(kb, qm_sc[h * rows : (h + 1) * rows, :]) * factor, LOW)
                for h in range(heads)
            ]
            m_old = m_sc[...]
            m_new = [
                jnp.maximum(m_old[h : h + 1, :], jnp.max(s[h], axis=0, keepdims=True))
                for h in range(heads)
            ]
            alpha = [jnp.exp2(m_old[h : h + 1, :] - m_new[h]) for h in range(heads)]
            p = [jnp.exp2(s[h] - m_new[h]) for h in range(heads)]
            sums = [jnp.sum(p[h], axis=0, keepdims=True) for h in range(heads)]
            pv = [nn(vt[span_of[h], :], p[h].astype(bf16)) for h in range(heads)]
            m_sc[...] = jnp.concatenate(m_new)
            l_sc[...] = l_sc[...] * jnp.concatenate(alpha) + jnp.concatenate(sums)
            for h in range(heads):
                acc_sc[span_of[h], :] = acc_sc[span_of[h], :] * alpha[h] + pv[h]

        return carry

    lax.fori_loop(0, kcount, step, 0)
    if closes:
        for h in range(heads):
            total = l_sc[h : h + 1, :]
            acc_sc[span_of[h], :] = jnp.where(real, acc_sc[span_of[h], :] / total, 0.0)
            lse_ref[h : h + 1, :] = jnp.where(real, m_sc[h : h + 1, :] + jnp.log2(total), -LOW)
        ctx_ref[...] = acc_sc[...].T.astype(bf16)
    else:
        m_out[...] = m_sc[...]
        l_out[...] = l_sc[...]
        acc_out[...] = acc_sc[...]


def whole(shape):
    return pl.BlockSpec(shape, lambda i, *_: (0,) * len(shape))


def attend(info, q, sources, offsets, kfirst, state=None, closes=False):
    rows, width = q.shape
    heads = width // HEAD_DIM
    keys = sum(source.shape[0] for source in sources)
    opens = state is None
    block = pl.BlockSpec((BLK, width), lambda i, *_: (i, 0))
    per_head = pl.BlockSpec((heads, BLK), lambda i, *_: (0, i))
    per_feature = pl.BlockSpec((width, BLK), lambda i, *_: (0, i))
    stats = jax.ShapeDtypeStruct((heads, rows), f32)
    carried = [per_head, per_head, per_feature]
    return pl.pallas_call(
        functools.partial(attend_kernel, heads, keys // BLK, kfirst, opens, closes, offsets),
        grid_spec=pltpu.PrefetchScalarGridSpec(
            num_scalar_prefetch=1,
            grid=(rows // BLK,),
            in_specs=[block]
            + [pl.BlockSpec(memory_space=pl.ANY)] * len(sources)
            + ([] if opens else carried),
            out_specs=[block, per_head] if closes else carried,
            scratch_shapes=[
                pltpu.VMEM((heads, BLK), f32),
                pltpu.VMEM((heads, BLK), f32),
                pltpu.VMEM((width, BLK), f32),
                pltpu.VMEM((heads * BLK, width), bf16),
                pltpu.VMEM((keys, width), bf16),
                pltpu.VMEM((keys, width), bf16),
                pltpu.VMEM((width, keys), bf16),
                pltpu.SemaphoreType.DMA((2 * len(sources),)),
            ],
        ),
        out_shape=[jax.ShapeDtypeStruct((rows, width), bf16), stats]
        if closes
        else [stats, stats, jax.ShapeDtypeStruct((width, rows), f32)],
        cost_estimate=pl.CostEstimate(flops=1024, bytes_accessed=1024, transcendentals=0),
        name="attend_near" if opens else "attend_far",
    )(info, q, *sources, *(() if opens else state))


def attend_back_kernel(
    heads, kcount, kfirst, offsets, info, q_ref, do_ref, o_ref, lse_ref, *refs
):
    count = len(offsets)
    sources, refs = refs[:count], refs[count:]
    dq_ref, *outs = refs[:5]
    dk_sc, dv_sc, dqt_sc, qm_sc, dom_sc, delta_sc, k_sc, v_sc, kt_sc, sems = refs[5:]
    i = pl.program_id(0)
    rows, width = q_ref.shape
    qbase = info[3 + i]
    first, last, real = row_limits(info, qbase, rows)
    low, high = key_range(info, qbase, rows)
    scale = 1.0 / math.sqrt(HEAD_DIM)
    factor = math.log2(math.e) * scale

    @pl.when(i == 0)
    def _():
        dk_sc[...] = jnp.zeros_like(dk_sc)
        dv_sc[...] = jnp.zeros_like(dv_sc)
        stage(sources, offsets, width, k_sc, v_sc, sems)
        transposed(k_sc, kt_sc, kcount)

    dqt_sc[...] = jnp.zeros_like(dqt_sc)
    do = do_ref[...]
    masked_heads(q_ref[...], qm_sc, heads)
    masked_heads(do, dom_sc, heads)
    prod = (do.astype(f32) * o_ref[...].astype(f32)).T
    span_of = [slice(h * HEAD_DIM, (h + 1) * HEAD_DIM) for h in range(heads)]
    rows_of = [slice(h * rows, (h + 1) * rows) for h in range(heads)]
    for h in range(heads):
        delta_sc[h : h + 1, :] = jnp.sum(prod[span_of[h], :], axis=0, keepdims=True)

    def step(j, carry):
        base = info[kfirst + j]

        @pl.when((base + BLK > low) & (base < high))
        def _():
            span = pl.ds(pl.multiple_of(j * BLK, BLK), BLK)
            kb = k_sc[span, :]
            vb = v_sc[span, :]
            kt = kt_sc[:, span]
            posk = base + lax.broadcasted_iota(jnp.int32, (BLK, rows), 0)
            allowed = (posk >= first) & (posk < last)
            s = [nt(kb, qm_sc[rows_of[h], :]) for h in range(heads)]
            dp = [nt(vb, dom_sc[rows_of[h], :]) for h in range(heads)]
            p = [
                jnp.where(allowed, jnp.exp2(s[h] * factor - lse_ref[0, h : h + 1, :]), 0.0)
                for h in range(heads)
            ]
            ds = [(p[h] * (dp[h] - delta_sc[h : h + 1, :])).astype(bf16) for h in range(heads)]
            low_p = [p[h].astype(bf16) for h in range(heads)]
            dv_sc[span, :] += nn(jnp.concatenate(low_p, axis=1), dom_sc[...])
            dk_sc[span, :] += nn(jnp.concatenate(ds, axis=1), qm_sc[...])
            for h in range(heads):
                dqt_sc[span_of[h], :] += nn(kt[span_of[h], :], ds[h])

        return carry

    lax.fori_loop(0, kcount, step, 0)
    dq_ref[...] = (dqt_sc[...] * scale).T.astype(bf16)

    @pl.when(i == pl.num_programs(0) - 1)
    def _():
        part = outs[0].shape[1]
        for n, out_ref in enumerate(outs):
            out_ref[0] = (dk_sc[n * part : (n + 1) * part, :] * scale).astype(bf16)
            out_ref[1] = dv_sc[n * part : (n + 1) * part, :].astype(bf16)


def attend_back(info, q, do, o, lse, sources, offsets, kfirst, pick, width):
    rows = q.shape[0]
    heads = width // HEAD_DIM
    keys = sum(source.shape[0] for source in sources)
    block = pl.BlockSpec((BLK, width), lambda i, *_: (i, pick))
    pair = (2, keys // 4, width)
    offsets = tuple((k_at + pick * width, v_at + pick * width) for k_at, v_at in offsets)
    return pl.pallas_call(
        functools.partial(attend_back_kernel, heads, keys // BLK, kfirst, offsets),
        grid_spec=pltpu.PrefetchScalarGridSpec(
            num_scalar_prefetch=1,
            grid=(rows // BLK,),
            in_specs=[
                block,
                block,
                block,
                pl.BlockSpec((1, heads, BLK), lambda i, *_: (pick, 0, i)),
            ]
            + [pl.BlockSpec(memory_space=pl.ANY)] * len(sources),
            out_specs=[pl.BlockSpec((BLK, width), lambda i, *_: (i, 0))] + [whole(pair)] * 4,
            scratch_shapes=[
                pltpu.VMEM((keys, width), f32),
                pltpu.VMEM((keys, width), f32),
                pltpu.VMEM((width, BLK), f32),
                pltpu.VMEM((heads * BLK, width), bf16),
                pltpu.VMEM((heads * BLK, width), bf16),
                pltpu.VMEM((heads, BLK), f32),
                pltpu.VMEM((keys, width), bf16),
                pltpu.VMEM((keys, width), bf16),
                pltpu.VMEM((width, keys), bf16),
                pltpu.SemaphoreType.DMA((2 * len(sources),)),
            ],
        ),
        out_shape=[jax.ShapeDtypeStruct((rows, width), bf16)]
        + [jax.ShapeDtypeStruct(pair, bf16)] * 4,
        cost_estimate=pl.CostEstimate(flops=1024, bytes_accessed=1024, transcendentals=0),
        name="attend_back",
    )(info, q, do, o, lse.reshape(-1, heads, rows), *sources)


def qkv_terms_kernel(order, *refs):
    rows, (dq_1, dq_2), pairs = refs[:8], refs[8:10], refs[10:18]
    sent_ref, mine_ref = refs[18:]
    size = rows[0].shape[0]
    query, key_value = None, None
    for n, rows_ref in enumerate(rows):
        left = rows_ref[...]
        span = slice((n % 2) * size, (n % 2 + 1) * size)
        first, second = pairs[n // 2 * 2], pairs[n // 2 * 2 + 1]
        grads = jnp.concatenate(
            [first[0, span], second[0, span], first[1, span], second[1, span]], axis=1
        )
        term = tn(left, grads)
        key_value = term if key_value is None else key_value + term
        if n < 2:
            term = tn(left, jnp.concatenate([dq_1[span], dq_2[span]], axis=1))
            query = term if query is None else query + term
    total = jnp.concatenate([query, key_value], axis=1)

    @pl.when(pl.program_id(0) == 0)
    def _():
        sent_ref[...] = total.astype(sent_ref.dtype)

    @pl.when(pl.program_id(0) == 1)
    def _():
        mine_ref[...] = total


def qkv_terms_of(rows, queries, pairs, order, sent_type):
    size, depth = rows[0].shape
    half = depth // 2
    wide = 2 * (queries[0].shape[1] + 2 * pairs[0].shape[2])
    return pl.pallas_call(
        qkv_terms_kernel,
        grid_spec=pltpu.PrefetchScalarGridSpec(
            num_scalar_prefetch=1,
            grid=(2,),
            in_specs=[pl.BlockSpec((size, half), lambda i, pick: (0, pick[i]))] * 8
            + [whole(x.shape) for x in (*queries, *pairs)],
            out_specs=[whole((half, wide)), whole((half, wide))],
        ),
        out_shape=[
            jax.ShapeDtypeStruct((half, wide), sent_type),
            jax.ShapeDtypeStruct((half, wide), f32),
        ],
        cost_estimate=pl.CostEstimate(flops=1024, bytes_accessed=1024, transcendentals=0),
        name="qkv_terms",
    )(order, *rows, *queries, *pairs)


def tp_swap(x, bit):
    return lax.ppermute(x, "tp", [(i, i ^ bit) for i in range(4)])


def gate_kernel(*refs):
    pass


def gate(through, *waits):
    through = tuple(through)
    anywhere = pl.BlockSpec(memory_space=pl.ANY)
    return pl.pallas_call(
        gate_kernel,
        in_specs=[anywhere] * (len(through) + len(waits)),
        out_specs=[anywhere] * len(through),
        out_shape=[jax.ShapeDtypeStruct(x.shape, x.dtype) for x in through],
        input_output_aliases={n: n for n in range(len(through))},
        name="gate",
    )(*through, *waits)


def tie(x, *others):
    for other in others:
        x = x + (other[(0,) * other.ndim].astype(f32) * 0.0).astype(x.dtype)
    return x


def fsdp_whole(shard, dim):
    if lax.axis_size("fsdp") != 2:
        full = lax.all_gather(shard, "fsdp", axis=dim, tiled=True)
        return full, full
    other = lax.ppermute(shard, "fsdp", [(0, 1), (1, 0)])
    low_half = lax.axis_index("fsdp") == 0
    return jnp.concatenate(
        [jnp.where(low_half, shard, other), jnp.where(low_half, other, shard)], axis=dim
    ), other


def fsdp_send(block_of, size, dim):
    if lax.axis_size("fsdp") != 2:
        mine = lax.psum_scatter(block_of(0, size), "fsdp", scatter_dimension=dim, tiled=True)
        return mine, jnp.zeros(mine.shape, bf16)
    half = size // 2
    place = lax.axis_index("fsdp")
    return block_of(place * half, half), block_of((1 - place) * half, half).astype(bf16)


def fsdp_swap(x):
    if lax.axis_size("fsdp") != 2:
        return x
    return lax.ppermute(x, "fsdp", [(0, 1), (1, 0)])


def ctx_swap(x, bit):
    return lax.ppermute(x, "ctx", [(i, i ^ bit) for i in range(4)])


def ctx_split(terms, bit):
    upper = (lax.axis_index("ctx") & bit) != 0
    size = terms.shape[0] // 2
    low_half, high_half = terms[:size], terms[size:]
    return (
        jnp.where(upper, high_half, low_half),
        jnp.where(upper, low_half, high_half).astype(bf16),
    )


def ctx_join(total, got, bit):
    upper = (lax.axis_index("ctx") & bit) != 0
    return jnp.concatenate([jnp.where(upper, got, total), jnp.where(upper, total, got)])


def rows_out(own):
    far = tp_swap(own, 2)
    near = tp_swap(own, 1)
    return own, near, far, tp_swap(far, 1)


def rows_in(terms):
    toward = terms[2] + tp_swap(terms[3].astype(bf16), 1).astype(f32)
    got = tp_swap(toward.astype(bf16), 2)
    here = terms[0] + tp_swap(terms[1].astype(bf16), 1).astype(f32)
    return here + got.astype(f32)


def natural(parts, core, y):
    r0, r1, r2, r3 = parts
    a0, a1 = jnp.where(core, r1, r0), jnp.where(core, r0, r1)
    a2, a3 = jnp.where(core, r3, r2), jnp.where(core, r2, r3)
    return jnp.concatenate(
        [jnp.where(y, a2, a0), jnp.where(y, a3, a1), jnp.where(y, a0, a2), jnp.where(y, a1, a3)]
    )


def norm_rows(rows):
    centre = rows - jnp.mean(rows, axis=-1, keepdims=True)
    inverse = lax.rsqrt(jnp.mean(centre * centre, axis=-1, keepdims=True) + norm_eps)
    return centre * inverse, inverse


def norm_back(grad, gain, normed, inverse):
    dn = grad * gain
    return (
        dn
        - jnp.mean(dn, axis=-1, keepdims=True)
        - normed * jnp.mean(dn * normed, axis=-1, keepdims=True)
    ) * inverse


def gelu_pair(values):
    phi_sum = 0.5 + 0.5 * lax.erf(values * math.sqrt(0.5))
    density = jnp.exp(values * values * -0.5) * (1.0 / math.sqrt(2.0 * math.pi))
    return (values * phi_sum).astype(bf16), phi_sum + values * density


def body(tokens, w_qkv, w_out, w_up, w_down, gains, shifts, lengths, out_grad):
    place = lax.axis_index("ctx")
    t = lax.axis_index("tp")
    core, y = (t & 1) == 1, (t >> 1) == 1
    tok_rows, depth = tokens.shape
    width = w_qkv.shape[2]
    quarter = tok_rows // 4
    order = (0, 2, 1, 3)

    def quarter_of(array, r):
        return lax.dynamic_slice_in_dim(array, (t ^ r) * quarter, quarter)

    half_a = jnp.concatenate([quarter_of(tokens, 0), quarter_of(tokens, 2)])
    left_a = lax.ppermute(half_a, "ctx", [(0, 1), (1, 2), (2, 3)])
    right_a = lax.ppermute(half_a, "ctx", [(3, 2), (2, 1), (1, 0)])
    half_b = jnp.concatenate([quarter_of(tokens, 1), quarter_of(tokens, 3)])
    far_left = lax.ppermute(left_a, "ctx", [(1, 2), (2, 3)])
    far_right = lax.ppermute(right_a, "ctx", [(2, 1), (1, 0)])
    full_qkv, got_qkv = fsdp_whole(w_qkv, 1)
    own_out, got_out = fsdp_whole(tie(w_out, got_qkv), 1)
    full_vectors, _ = fsdp_whole(jnp.concatenate([tie(gains, got_qkv), shifts]), 1)
    full_up, got_up = fsdp_whole(tie(w_up, got_qkv), 0)
    full_down, got_down = fsdp_whole(tie(w_down, got_qkv), 1)
    full_vectors = full_vectors.astype(f32)
    gain = full_vectors[:2]
    shift = full_vectors[2:]

    positions = jnp.stack([t ^ r for r in order]) * quarter
    chunks = jnp.stack([place, place - 1, place + 1, place ^ 2]) * tok_rows
    info = jnp.concatenate(
        [
            jnp.cumsum(lengths[0]),
            place * tok_rows + positions,
            (chunks[:, None] + positions[None, :]).reshape(-1),
        ]
    ).astype(jnp.int32)

    w_q, w_k, w_v = full_qkv[0], full_qkv[1], full_qkv[2]
    w_all = jnp.concatenate([w_q, w_k, w_v], axis=1)
    w_kv = w_all[:, width:]
    own = [nn(rows, w_all).astype(bf16) for rows in (half_a, half_b)]
    left_b, right_b = tp_swap(left_a, 1), tp_swap(right_a, 1)
    near = [nn(rows, w_kv).astype(bf16) for rows in (left_a, left_b, right_a, right_b)]
    queries = jnp.concatenate([part[:, :width] for part in own])
    own_at, other_at = (width, 2 * width), (0, width)
    near_at = (own_at,) * 2 + (other_at,) * 4
    state = attend(info, queries, own + near, near_at, 7)
    out_y = tp_swap(own_out, 2)
    out_rows = (own_out, out_y, tp_swap(own_out, 1), tp_swap(out_y, 1))
    far_left, far_right = gate((far_left, far_right), state[0], got_up, got_down, *out_rows)
    far_a = jnp.where(place >= 2, far_left, far_right)
    far_b = tp_swap(far_a, 1)
    far = [nn(rows, w_kv).astype(bf16) for rows in (far_a, far_b)]
    context, log_totals = attend(info, queries, far, (other_at,) * 2, 19, state, True)

    pieces = jnp.split(context, 4)
    arrived = [pieces[0]] + [tp_swap(pieces[n], order[n]) for n in (1, 2, 3)]
    resid_rows = quarter_of(tokens, 0).astype(f32)
    for piece, rows in zip(arrived, out_rows):
        resid_rows = resid_rows + nn(piece, rows)
    normed_first, inverse_first = norm_rows(resid_rows)
    hidden = normed_first * gain[0] + shift[0]
    hid0 = hidden.astype(bf16)
    hid2, hid1 = tp_swap(hid0, 2), tp_swap(hid0, 1)
    hid_near = jnp.concatenate([hid0, hid1])
    act_near, slope_near = gelu_pair(nn(hid_near, full_up))
    terms_near = nn(act_near, full_down)
    hid2, terms_near = gate((hid2, terms_near))
    hid_far = jnp.concatenate([hid2, tp_swap(hid2, 1)])
    act_far, slope_far = gelu_pair(nn(hid_far, full_up))
    terms_far = nn(act_far, full_down)
    ffn_rows = rows_in(
        (terms_near[:quarter], terms_near[quarter:], terms_far[:quarter], terms_far[quarter:])
    )
    normed_second, inverse_second = norm_rows(hidden + ffn_rows)
    result = (normed_second * gain[1] + shift[1]).astype(bf16)
    grad_rows = quarter_of(out_grad, 0).astype(f32)
    grad_mid = norm_back(grad_rows, gain[1], normed_second, inverse_second)

    mid0 = grad_mid.astype(bf16)
    mid2, mid1 = tp_swap(mid0, 2), tp_swap(mid0, 1)
    mid_near = jnp.concatenate([mid0, mid1])
    pre_near = (nt(mid_near, full_down) * slope_near).astype(bf16)
    terms_near = nt(pre_near, full_up)
    mid2, terms_near = gate((mid2, terms_near))
    mid_far = jnp.concatenate([mid2, tp_swap(mid2, 1)])

    def column_block(*pairs):
        return lambda start, size: sum(
            tn(left, lax.dynamic_slice_in_dim(right, start, size, axis=1)) for left, right in pairs
        )

    def row_block(*pairs):
        return lambda start, size: sum(
            tn(lax.dynamic_slice_in_dim(left, start, size, axis=1), right) for left, right in pairs
        )

    down_terms, down_send = fsdp_send(
        column_block((act_near, mid_near), (act_far, mid_far)), depth, 1
    )
    down_got = fsdp_swap(down_send)

    pre_far = (nt(mid_far, full_down) * slope_far).astype(bf16)
    terms_far = nt(pre_far, full_up)
    hidden_grad = grad_mid + rows_in(
        (terms_near[:quarter], terms_near[quarter:], terms_far[:quarter], terms_far[quarter:])
    )
    up_terms, up_send = fsdp_send(row_block((hid_near, pre_near), (hid_far, pre_far)), depth, 0)
    resid_grad = norm_back(hidden_grad, gain[0], normed_first, inverse_first)
    attn_own = resid_grad.astype(bf16)

    up_send, down_got = gate((up_send, down_got), attn_own)
    up_got = fsdp_swap(up_send)
    down_terms = down_terms + down_got.astype(f32)
    share = up_terms.shape[0]
    down_terms = jnp.concatenate(jnp.split(down_terms, depth // share), axis=1)
    down_kept, send = ctx_split(down_terms, 1)
    down_got = ctx_swap(send, 1)
    pieces = [nt(attn_own, rows).astype(bf16) for rows in out_rows]
    context_grad = jnp.concatenate(
        [pieces[0]] + [tp_swap(pieces[n], order[n]) for n in (1, 2, 3)]
    )

    vectors = jnp.stack(
        [
            jnp.sum(hidden_grad * normed_first, axis=0),
            jnp.sum(grad_rows * normed_second, axis=0),
            jnp.sum(hidden_grad, axis=0),
            jnp.sum(grad_rows, axis=0),
        ]
    )
    spread = jnp.concatenate(
        [attn_own, result, jnp.pad(vectors, ((0, PAD_ROWS - 4), (0, 0))).astype(bf16)]
    )
    context_grad, spread = gate((context_grad, spread))
    spread_far, spread_near = tp_swap(spread, 2), tp_swap(spread, 1)

    sources = own + near + far
    sources_at = (own_at,) * 2 + (other_at,) * 6
    part = width // 2
    dq_1, own_1, left_1, right_1, far_1 = attend_back(
        info, queries, context_grad, context, log_totals, sources, sources_at, 7, 0, part
    )
    info_2, far_1, left_1, right_1, down_got, up_got, spread_far = gate(
        (info, far_1, left_1, right_1, down_got, up_got, spread_far), spread_near
    )
    spread_both = tp_swap(spread_far, 1)

    def home(left_kv, right_kv, far_kv):
        return (
            ctx_swap(far_kv, 2),
            lax.ppermute(left_kv, "ctx", [(3, 2), (2, 1), (1, 0)]),
            lax.ppermute(right_kv, "ctx", [(0, 1), (1, 2), (2, 3)]),
        )

    home_1 = home(left_1, right_1, far_1)
    up_kept, up_send = ctx_split(up_terms + up_got.astype(f32), 1)
    down_kept, down_send = ctx_split(down_kept + down_got.astype(f32), 2)
    info_2, up_send, down_send = gate((info_2, up_send, down_send), spread_both)
    up_got = ctx_swap(up_send, 1)
    down_got = ctx_swap(down_send, 2)

    dq_2, own_2, left_2, right_2, far_2 = attend_back(
        info_2, queries, context_grad, context, log_totals, sources, sources_at, 7, 1, part
    )
    (
        far_2, left_2, right_2, down_got, up_got, *home_1,
        own_1, own_2, dq_1, dq_2, left_1, right_1, far_1,
        spread, spread_near, spread_far, spread_both,
    ) = gate(
        (
            far_2, left_2, right_2, down_got, up_got, *home_1,
            own_1, own_2, dq_1, dq_2, left_1, right_1, far_1,
            spread, spread_near, spread_far, spread_both,
        )
    )
    home_2 = home(left_2, right_2, far_2)
    down_total = lax.optimization_barrier((down_kept + down_got.astype(f32)).astype(bf16))
    up_kept, send = ctx_split(up_kept + up_got.astype(f32), 2)
    ffn_got = ctx_swap(jnp.concatenate([down_total, send]), 2)

    def spread_sums(held):
        return (
            jnp.concatenate([held[n][:quarter] for n in order]),
            sum(x[2 * quarter :].astype(f32) for x in held),
        )

    def rest_of(qkv_terms, start, size):
        right = lax.dynamic_slice_in_dim(attn_all, start, size, axis=1)
        extra = lax.dynamic_slice_in_dim(vectors, start, size, axis=1)
        rows = qkv_terms.shape[0]
        terms = tn(context, right).astype(qkv_terms.dtype).reshape(rows, -1)
        terms = jnp.concatenate([qkv_terms, terms], axis=1)
        extra = jnp.pad(extra, ((0, PAD_ROWS), (0, terms.shape[1] - size)))
        return jnp.concatenate([terms, extra.astype(terms.dtype)])

    pairs = (own_1, own_2, left_1, left_2, right_1, right_2, far_1, far_2)
    rows = (half_a, half_b, left_a, left_b, right_a, right_b, far_a, far_b)
    if lax.axis_size("fsdp") == 2:
        mine = lax.axis_index("fsdp")
        picks = jnp.stack([1 - mine, mine]).astype(jnp.int32)
        half = depth // 2
        qkv_send, qkv_terms = qkv_terms_of(rows, (dq_1, dq_2), pairs, picks, bf16)
        spread, spread_near, spread_far, spread_both = gate(
            (spread, spread_near, spread_far, spread_both), qkv_send
        )
        held = (spread, spread_near, spread_far, spread_both)
        attn_all, vectors = spread_sums(held)
        rest_got = fsdp_swap(rest_of(qkv_send, (1 - mine) * half, half))
        rest = rest_of(qkv_terms, mine * half, half)
    else:
        halves = qkv_terms_of(rows, (dq_1, dq_2), pairs, jnp.arange(2, dtype=jnp.int32), f32)
        qkv_terms = lax.psum_scatter(
            jnp.concatenate(halves), "fsdp", scatter_dimension=0, tiled=True
        )
        held = (spread, spread_near, spread_far, spread_both)
        attn_all, vectors = spread_sums(held)
        out_terms = lax.psum_scatter(
            jnp.concatenate([tn(context, attn_all), vectors]), "fsdp",
            scatter_dimension=1, tiled=True,
        )
        rest = jnp.concatenate(
            [qkv_terms, out_terms[:width].reshape(qkv_terms.shape[0], -1)], axis=1
        )
        extra = out_terms[width:]
        extra = jnp.pad(extra, ((0, PAD_ROWS), (0, rest.shape[1] - extra.shape[1])))
        rest = jnp.concatenate([rest, extra])
        rest_got = jnp.zeros(rest.shape, bf16)
    result_parts = [x[quarter : 2 * quarter] for x in held]
    query_grad = jnp.concatenate([dq_1, dq_2], axis=1)

    def owned(own_kv, arrivals):
        total = own_kv.astype(f32)
        for arrival in arrivals:
            total = total + arrival.astype(f32)
        return total.astype(bf16)

    total_1 = owned(own_1, home_1)
    input_terms = (
        nt(query_grad, w_q) + nt(total_1[0], w_k[:, :part]) + nt(total_1[1], w_v[:, :part])
    )
    *home_2, rest_got, ffn_got = gate((*home_2, rest_got, ffn_got), input_terms)
    down_got, up_got = jnp.split(ffn_got, 2)
    total_2 = owned(own_2, home_2)
    terms = input_terms + nt(total_2[0], w_k[:, part:]) + nt(total_2[1], w_v[:, part:])
    q0, q2, q1, q3 = jnp.split(terms, 4)
    toward = q2 + tp_swap(q3.astype(bf16), 1).astype(f32)
    input_got = tp_swap(toward.astype(bf16), 2)
    here = q0 + tp_swap(q1.astype(bf16), 1).astype(f32)
    up_total = lax.optimization_barrier((up_kept + up_got.astype(f32)).astype(bf16))
    up_got = ctx_swap(up_total, 2)
    out_shape = (width, depth // lax.axis_size("fsdp"))
    rest = rest + rest_got.astype(f32)
    fourth = rest.shape[0] // 4

    def fourth_of(shift):
        return lax.dynamic_slice_in_dim(rest, (place ^ shift) * fourth, fourth)

    rest_kept = fourth_of(0)
    rest_got = [ctx_swap(fourth_of(shift).astype(bf16), shift) for shift in (1, 2, 3)]

    input_got, up_got, *rest_got = gate((input_got, up_got, *rest_got))
    input_own = (resid_grad + here + input_got.astype(f32)).astype(bf16)
    input_far, input_near = tp_swap(input_own, 2), tp_swap(input_own, 1)
    for got in rest_got:
        rest_kept = rest_kept + got.astype(f32)
    rest_total = lax.optimization_barrier(rest_kept.astype(bf16))
    rest_parts = (rest_total, *(ctx_swap(rest_total, shift) for shift in (1, 2, 3)))
    ffn_total = jnp.concatenate(
        [ctx_join(down_total, down_got, 2), ctx_join(up_total, up_got, 2)]
    )
    ffn_got = ctx_swap(ffn_total, 1)
    input_parts = (input_own, input_near, input_far, tp_swap(input_far, 1))
    down_grad, up_grad = (
        ctx_join(total, got, 1).astype(f32)
        for total, got in zip(jnp.split(ffn_total, 2), jnp.split(ffn_got, 2))
    )
    down_grad = jnp.concatenate(jnp.split(down_grad, depth // down_grad.shape[0], axis=1))
    rest_total = natural(rest_parts, (place & 1) == 1, (place >> 1) == 1).astype(f32)
    qkv_grad = jnp.stack([rest_total[:share, n * width : (n + 1) * width] for n in range(3)])
    out_proj_grad = rest_total[:share, 3 * width :].reshape(out_shape)
    vectors = rest_total[share : share + 4, : out_shape[1]]
    return (
        natural(result_parts, core, y),
        natural(input_parts, core, y),
        qkv_grad,
        out_proj_grad,
        up_grad,
        down_grad,
        vectors[:2],
        vectors[2:],
    )


def solution(mesh):
    return jax.shard_map(
        body,
        mesh=mesh,
        in_specs=(
            P(("fsdp", "ctx"), None),
            P(None, "fsdp", "tp"),
            P("tp", "fsdp"),
            P("fsdp", "tp"),
            P("tp", "fsdp"),
            P(None, "fsdp"),
            P(None, "fsdp"),
            P("fsdp", None),
            P(("fsdp", "ctx"), None),
        ),
        out_specs=(
            P(("fsdp", "ctx"), None),
            P(("fsdp", "ctx"), None),
            P(None, "fsdp", "tp"),
            P("tp", "fsdp"),
            P("fsdp", "tp"),
            P("tp", "fsdp"),
            P(None, "fsdp"),
            P(None, "fsdp"),
        ),
        check_vma=False,
    )
```
